1024 devices in a mesh: axial: 64 (over x, z), azim: 16 (over y, core).
Axes of the slice: x: 8, y: 8, z: 8, core: 2. Of those that a mesh axis runs over, the one named last changes fastest.
Arguments:
- gas_fields: float32 [3, 1024, 128, 128], P(None, 'axial', 'azim'), may hold values from -4 to 4
- drop_mass: float32 [2097152], P(('axial', 'azim')), may hold values from 0.2 to 2
- drop_temp: float32 [2097152], P(('axial', 'azim')), may hold values from -4 to 4
- drop_speed: float32 [2097152], P(('axial', 'azim')), may hold values from -4 to 4
- dest_first: int32 [2097152, 1], P(('axial', 'azim')), may hold values from 0 to 15; in each aligned block of 2048 rows (0 to 2047, 2048 to 4095, ...) at most 256 rows name the same one
- cell_first: int32 [2097152], P(('axial', 'azim')), may hold values from 0 to 16383
- dest_second: int32 [4194304, 1], P(('axial', 'azim')), may hold values from 0 to 15; in each aligned block of 4096 rows (0 to 4095, 4096 to 8191, ...) at most 256 rows name the same one
- cell_second: int32 [4194304], P(('axial', 'azim')), may hold values from 0 to 16383
Outputs:
- gas_next: float32 [3, 1024, 128, 128], P(None, 'axial', 'azim')
- drop_records: float32 [6, 4194304], P(None, ('axial', 'azim'))
The draws below stay inside these ranges and needn't reach their ends.
Inputs may be any that keep to these rules, and one draw needn't show every extreme that they name: `dest_first`: in the rows of one device (aligned blocks of 2048 rows) no sector is named by more than 256 rows. `dest_second`: in the rows of one device (aligned blocks of 4096 rows) no sector is named by more than 256 rows. `cell_first`: local cell index (z * 8 + a) * 128 + r within the block of the device that holds the row. `cell_second`: local cell index (z * 8 + a) * 128 + r within the block of the device that holds the slot.
All inputs are finite; a program needn't handle non-finite values.
Results may differ from the reference program's by a relative error of at most 0.0003.
Values sent between devices are 32-bit elements; how exact they have to be, the bound alone decides.
No kernel may reach another device: no remote copies, remote signals or barrier semaphores. Data moves between devices by JAX's collectives and lax.ppermute only.
A program may use at most 32 MiB of HBM per device.

```python
import math
import jax
import jax.numpy as jnp
import numpy as np
from jax import lax

R = 128
CA = 8
CZ = 16
P_DEV = 2048
NA = 128
NZ = 1024
CELLS_DEV = 16384
CAP1 = 256
CAP2 = 256
DROPS = 2097152
SLOTS1 = 4194304
N_AXIAL = 64
N_AZIM = 16


def with_ends(values, stream_key, low, high):
    index_at = [jax.random.randint(jax.random.fold_in(stream_key, axis), (), 0, length) for axis, length in enumerate(values.shape)]
    main_axis = values.shape.index(max(values.shape))
    beside = index_at[:main_axis] + [(index_at[main_axis] + 1) % values.shape[main_axis]] + index_at[main_axis + 1:]
    return values.at[tuple(index_at)].set(low).at[tuple(beside)].set(high)


def block_scale(rng, extent, split, smallest, top_value):
    def one(dim, shards_of):
        steps = jax.random.uniform(jax.random.fold_in(jax.random.fold_in(rng, 6), dim), (shards_of,), jnp.float32, smallest / len(split), top_value / len(split))
        return jnp.repeat(jnp.exp(steps), extent[dim] // shards_of).reshape((-1,) + (1,) * (len(extent) - dim - 1))

    factor_of = one(*split[0])
    for cut in split[1:]:
        factor_of = factor_of * one(*cut)
    return factor_of


def deal_out(own_key, own, number, rows, count, top, bound, lean):
    ranking = jax.random.permutation(own_key, count)
    heavy_load, usual = portions_of(count, rows * top, bound, lean, True), portions_of(count, rows * top, bound, lean, False)
    places = jnp.arange(count)

    def named(lengths, rotation):
        used = int((lengths > 0).sum())
        fixed = max(1, used // 4)
        passed = fixed + (places - fixed + rotation * (used - fixed)) % max(1, count - fixed)
        return jnp.zeros((count,), jnp.int32).at[ranking[jnp.where(places < fixed, places, passed)]].set(jnp.asarray(lengths, jnp.int32))

    lengths = jnp.where(number % 4 == 0, named(heavy_load, number // 4), named(usual, number - number // 4 - 1))
    mixed = jax.random.permutation(jax.random.fold_in(own, 3), count)
    donor, taker = mixed[0:count // 2 * 2:2], mixed[1:count // 2 * 2:2]
    slack = jnp.minimum(lengths[donor] - 1, bound - lengths[taker]) // 2
    slack = jnp.where((donor == ranking[0]) | (taker == ranking[0]) | (lengths[taker] == 0), 0, jnp.maximum(slack, 0))
    passed = jax.random.randint(jax.random.fold_in(own, 4), (count // 2,), 0, 1 << 20) % (slack + 1)
    lengths = lengths.at[donor].add(-passed).at[taker].add(passed)
    members = jnp.searchsorted(jnp.cumsum(lengths), jnp.arange(rows * top), side="right").astype(jnp.int32)
    grid = members.reshape(top, rows).T
    grid = grid[jax.random.permutation(jax.random.fold_in(own, 1), rows)]
    rotation = jax.random.randint(jax.random.fold_in(own, 2), (rows, 1), 0, top)
    return jnp.take_along_axis(grid, (jnp.arange(top)[None, :] + rotation) % top, axis=1)


def portions_of(count, total, most, slope, full):
    loads = [(1 << 20) // math.isqrt(grade ** slope) + 1 for grade in range(1, count + 1)]
    largest = most if full else min(most, max(-(-total // count), total * loads[0] // sum(loads)))
    least = 1 if total - largest >= count - 1 else 0
    counts, surplus = [largest] + [least] * (count - 1), total - largest - least * (count - 1)
    while surplus > 0:
        movable = [i for i in range(1, count) if counts[i] < largest] or [i for i in range(1, count) if counts[i] < most]
        pool, remaining = sum([loads[i] for i in movable]), surplus
        for i in movable:
            more = min(most - counts[i], max(1, remaining * loads[i] // pool), surplus)
            counts[i] = counts[i] + more
            surplus = surplus - more
    return np.array(counts)


def noise(stream_key, extent, width, limit, cuts=(), kind=jnp.bfloat16):
    level = block_scale(stream_key, extent, cuts, -0.22, 0.18) if cuts else 1.0
    drawn = jax.random.normal(stream_key, extent, jnp.float32) * width * level
    return jnp.minimum(jnp.maximum(drawn, -limit), limit).astype(kind)


def setup_inputs(seed: int = 0) -> dict:
    streams_of = jax.random.split(jax.random.key(seed), 9)
    gas_fields = noise(streams_of[0], (3, NZ, NA, R), 1.0, 4.0, ((1, 64), (2, 16)), jnp.float32)
    drop_mass = jnp.clip(jnp.exp(math.log(2.0) - 2.3025851 * jax.random.uniform(streams_of[1], (DROPS,), jnp.float32) ** block_scale(streams_of[1], (DROPS,), ((0, 1024),), -0.2, 0.2)), 0.2, 2.0)
    drop_temp = noise(streams_of[2], (DROPS,), 1.0, 4.0, ((0, 1024),), jnp.float32)
    drop_speed = noise(streams_of[3], (DROPS,), 1.0, 4.0, ((0, 1024),), jnp.float32)
    dest_first_keys = jax.random.split(jax.random.fold_in(streams_of[4], 1), DROPS // P_DEV)
    dest_first_turns = jax.random.permutation(jax.random.fold_in(streams_of[4], 3), DROPS // P_DEV)
    dest_first = jax.vmap(lambda own, number: deal_out(jax.random.fold_in(streams_of[4], 2), own, number, P_DEV, N_AZIM, 1, CAP1, 2))(dest_first_keys, dest_first_turns).reshape((DROPS, 1))
    cell_first = with_ends(jax.random.randint(streams_of[5], (DROPS,), 0, CELLS_DEV), jax.random.fold_in(streams_of[5], 1), 0, CELLS_DEV - 1).astype(jnp.int32)
    dest_second_keys = jax.random.split(jax.random.fold_in(streams_of[6], 1), SLOTS1 // (N_AZIM * CAP1))
    dest_second_turns = jax.random.permutation(jax.random.fold_in(streams_of[6], 3), SLOTS1 // (N_AZIM * CAP1))
    dest_second = jax.vmap(lambda own, number: deal_out(jax.random.fold_in(streams_of[6], 2), own, number, N_AZIM * CAP1, N_AZIM, 1, CAP2, 2))(dest_second_keys, dest_second_turns).reshape((SLOTS1, 1))
    cell_second = with_ends(jax.random.randint(streams_of[7], (SLOTS1,), 0, CELLS_DEV), jax.random.fold_in(streams_of[7], 1), 0, CELLS_DEV - 1).astype(jnp.int32)
    return dict(gas_fields=gas_fields, drop_mass=drop_mass, drop_temp=drop_temp, drop_speed=drop_speed, dest_first=dest_first, cell_first=cell_first, dest_second=dest_second, cell_second=cell_second)


DT_STEP = 0.01
TAU_HEAT = 0.04
TAU_MASS = 0.05
TAU_DRAG = 0.03
LATENT = 0.5
COUPLING = 1.0
FORCING = 4.0
ADVECT = 0.16
RADIUS_FLOOR = 0.7
DIFFUSION = (0.2, 0.15, 0.17)
WALL_VALUES = (1.0, 0.0, 0.0)


def increment(fields, z_next, z_prev, a_next, a_prev, opposite, sources, aspect):
    radial_count = fields.shape[3]
    wall_all = jnp.asarray(WALL_VALUES, jnp.float32).reshape(3, 1, 1, 1)
    radial_pad = jnp.concatenate([opposite[..., 1:2], opposite[..., 0:1], fields, 2.0 * wall_all - fields[..., -1:], 2.0 * wall_all - fields[..., -2:-1]], axis=3)
    minus_two = radial_pad[..., 0:radial_count]
    minus_one = radial_pad[..., 1:radial_count + 1]
    plus_one = radial_pad[..., 3:radial_count + 3]
    plus_two = radial_pad[..., 4:radial_count + 4]
    radial_pos = jnp.arange(radial_count, dtype=jnp.float32) + 0.5
    inverse = 1.0 / (12.0 * radial_pos)
    geometry = aspect * aspect / jnp.maximum(radial_pos / radial_count, RADIUS_FLOOR) ** 2
    laplace = (-plus_two + 16.0 * plus_one - 30.0 * fields + 16.0 * minus_one - minus_two) / 12.0
    laplace = laplace + (-plus_two + 8.0 * plus_one - 8.0 * minus_one + minus_two) * inverse
    laplace = laplace + geometry * (a_next + a_prev - 2.0 * fields)
    laplace = laplace + (z_next + z_prev - 2.0 * fields) / 16.0
    kappa_all = jnp.asarray(DIFFUSION, jnp.float32).reshape(3, 1, 1, 1)
    forcing_all = jnp.asarray((0.0, 0.0, FORCING), jnp.float32).reshape(3, 1, 1, 1)
    return kappa_all * laplace - ADVECT * fields[2:3] * (z_next - z_prev) + DT_STEP * (sources + forcing_all)


def droplet_terms(flat_gas, states, live_flag, cells):
    sample_gas = jnp.take(flat_gas, cells, axis=1)
    drop_mass = states[0]
    excess = 0.3 + 0.2 * jnp.tanh(states[1]) - sample_gas[1]
    evaporate = drop_mass * excess / TAU_MASS
    heating = sample_gas[0] - states[1]
    drag_diff = sample_gas[2] - states[2]
    change = jnp.stack([-evaporate, heating / TAU_HEAT - LATENT * excess / TAU_MASS, drag_diff / TAU_DRAG]) * live_flag
    source_terms = jnp.stack([-COUPLING * drop_mass * heating / TAU_HEAT, COUPLING * evaporate, -COUPLING * drop_mass * drag_diff / TAU_DRAG])
    deposit = jnp.zeros_like(flat_gas).at[:, cells].add(source_terms)
    return change, deposit


def slot_ranks(targets, sectors):
    matches = (targets[:, None] == jnp.arange(sectors, dtype=jnp.int32)[None, :]).astype(jnp.int32)
    running = jnp.cumsum(matches, axis=0).astype(jnp.int32) - 1
    return jnp.sum(running * matches, axis=1).astype(jnp.int32)


def tendency(fields, sources):
    aspect = NA / (2.0 * math.pi * R)
    padded = jnp.concatenate([fields[:, -1:], fields, fields[:, :1]], axis=1)

    def slab_term(block_id):
        start_at = (block_id * CZ).astype(jnp.int32)
        planes = lax.dynamic_slice_in_dim(padded, start_at, CZ + 2, 1)
        middle = planes[:, 1:-1]
        local_src = lax.dynamic_slice_in_dim(sources, start_at, CZ, 1)
        opposite = jnp.roll(middle[..., :2], NA // 2, axis=2)
        return increment(middle, planes[:, 2:], planes[:, :-2], jnp.roll(middle, -1, 2), jnp.roll(middle, 1, 2), opposite, local_src, aspect)

    pieces = lax.map(slab_term, jnp.arange(N_AXIAL, dtype=jnp.int32))
    return jnp.moveaxis(pieces, 0, 1).reshape(fields.shape)


def global_cells(cells, rows_dev):
    owner_dev = jnp.arange(cells.shape[0], dtype=jnp.int32) // rows_dev
    axial_block = owner_dev // N_AZIM
    sector = owner_dev % N_AZIM
    plane_at = cells // (CA * R)
    column = (cells // R) % CA
    radial = cells % R
    return ((axial_block * CZ + plane_at) * NA + sector * CA + column) * R + radial


def migrate(records, targets, capacity, rows_dev):
    total_rows = records.shape[1]
    devices_all = total_rows // rows_dev
    grouped = targets[:, 0].reshape(devices_all, rows_dev)

    def ranks_of(targets_row):
        return slot_ranks(targets_row, N_AZIM)

    ranks = lax.map(ranks_of, grouped)
    sender = jnp.arange(devices_all, dtype=jnp.int32)[:, None]
    position = (((sender // N_AZIM) * N_AZIM + grouped) * N_AZIM + sender % N_AZIM) * capacity + ranks
    empty = jnp.zeros((records.shape[0], devices_all * N_AZIM * capacity), jnp.float32)
    return empty.at[:, position.reshape(-1)].set(records)


def reference(gas_fields, drop_mass, drop_temp, drop_speed, dest_first, cell_first, dest_second, cell_second):
    cap_first = 2 * P_DEV // N_AZIM
    cap_second = cap_first
    state_start = jnp.stack([drop_mass, drop_temp, drop_speed])
    live_start = (drop_mass > 0).astype(jnp.float32)
    change_first, deposit_first = droplet_terms(gas_fields.reshape(3, -1), state_start, live_start, global_cells(cell_first, P_DEV))
    gas_middle = gas_fields + tendency(gas_fields, deposit_first.reshape(gas_fields.shape))
    state_middle = state_start + DT_STEP * change_first
    moved = migrate(jnp.concatenate([state_middle, state_start], axis=0), dest_first, cap_first, P_DEV)
    state_now = moved[:3]
    state_anchor = moved[3:]
    live_now = (state_anchor[0] > 0).astype(jnp.float32)
    rows_second = N_AZIM * cap_first
    change_second, deposit_second = droplet_terms(gas_middle.reshape(3, -1), state_now, live_now, global_cells(cell_second, rows_second))
    gas_next = 0.75 * gas_fields + 0.25 * (gas_middle + tendency(gas_middle, deposit_second.reshape(gas_fields.shape)))
    state_final = 0.75 * state_anchor + 0.25 * (state_now + DT_STEP * change_second)
    drop_records = migrate(jnp.concatenate([state_final, state_anchor], axis=0), dest_second, cap_second, rows_second)
    return gas_next, drop_records
```

```python
import math

import jax
import jax.numpy as jnp
from jax import lax
from jax.experimental import pallas as pl
from jax.experimental.pallas import tpu as pltpu
from jax.sharding import PartitionSpec as P

DT_STEP = 0.01
TAU_HEAT = 0.04
TAU_MASS = 0.05
TAU_DRAG = 0.03
LATENT = 0.5
COUPLING = 1.0
FORCING = (0.0, 0.0, 4.0)
ADVECT = 0.16
RADIUS_FLOOR = 0.7
DIFFUSION = (0.2, 0.15, 0.17)
WALL_VALUES = (1.0, 0.0, 0.0)

F32 = jnp.float32
BF16 = jnp.bfloat16
LANES = 128
SUB = 8
VMEM_LIMIT = 40 << 20


def iota(shape, dim):
    return lax.broadcasted_iota(jnp.int32, shape, dim)


def one_hot(row, size):
    hit = iota((size, row.shape[1]), 0) == row
    return jnp.where(hit, 1.0, 0.0).astype(BF16)


def halves(x):
    head = x.astype(BF16)
    return head, (x - head.astype(F32)).astype(BF16)


def wide_row(ref, j):
    return jnp.concatenate([ref[pl.ds(j, 1), :], ref[pl.ds(j + 1, 1), :]], axis=1)


def dot_nt(a, b):
    return lax.dot_general(a, b, (((1,), (1,)), ((), ())), preferred_element_type=F32)


def gas_table(planes):
    turned = [p.T for p in planes]
    parts = [jnp.concatenate(halves(t), axis=1) for t in turned]
    return jnp.concatenate(parts, axis=0), turned


def sample(table, cell_ref, out_ref):
    size = table.shape[1] // 2
    lanes_r = table.shape[0] // 3
    shift = lanes_r.bit_length() - 1
    for j in range(0, cell_ref.shape[0], 2):
        cell = wide_row(cell_ref, j)
        pick = one_hot(cell >> shift, size)
        mixed = jnp.dot(table, jnp.concatenate([pick, pick], axis=0), preferred_element_type=F32)
        here = iota((lanes_r, cell.shape[1]), 0) == (cell & (lanes_r - 1))
        for c in range(3):
            part = jnp.where(here, mixed[c * lanes_r : (c + 1) * lanes_r], 0.0)
            row = jnp.sum(part, axis=0, keepdims=True)
            out_ref[c, pl.ds(j, 1), :] = row[:, :LANES]
            out_ref[c, pl.ds(j + 1, 1), :] = row[:, LANES:]


def droplet_rates(states, gas, live):
    mass, temp, speed = states
    excess = 0.3 + 0.2 * jnp.tanh(temp) - gas[1]
    evaporate = mass * excess / TAU_MASS
    heating = gas[0] - temp
    drag = gas[2] - speed
    change = (
        -evaporate * live,
        (heating / TAU_HEAT - LATENT * excess / TAU_MASS) * live,
        drag / TAU_DRAG * live,
    )
    source = (
        -COUPLING * mass * heating / TAU_HEAT,
        COUPLING * evaporate,
        -COUPLING * mass * drag / TAU_DRAG,
    )
    return change, source


def deposit(source_ref, cell_ref, rows, lanes_r):
    shift = lanes_r.bit_length() - 1
    total = None
    for j in range(0, cell_ref.shape[0], 2):
        cell = wide_row(cell_ref, j)
        pick = one_hot(cell >> shift, rows)
        here = iota((lanes_r, cell.shape[1]), 0) == (cell & (lanes_r - 1))
        spread = []
        for c in range(3):
            parts = halves(wide_row(source_ref.at[c], j))
            spread.append(
                jnp.concatenate(
                    [jnp.where(here, p.astype(F32), 0.0).astype(BF16) for p in parts], axis=1
                )
            )
        piece = dot_nt(jnp.concatenate([pick, pick], axis=1), jnp.concatenate(spread, axis=0))
        total = piece if total is None else total + piece
    return total


def slot_of(dest, sectors, capacity):
    n = dest.shape[0]
    hits = jnp.concatenate(
        [jnp.where(dest == t, 1.0, 0.0) for t in range(sectors)], axis=0
    ).astype(BF16)
    upto = jnp.where(iota((LANES, LANES), 0) <= iota((LANES, LANES), 1), 1.0, 0.0).astype(BF16)
    inside = jnp.dot(hits, upto, preferred_element_type=F32)
    every = jnp.dot(hits, jnp.ones((LANES, LANES), BF16), preferred_element_type=F32)
    before = jnp.where(iota((n, n), 1) < iota((n, n), 0), 1.0, 0.0).astype(BF16)
    rank = jnp.zeros(dest.shape, F32)
    for t in range(sectors):
        rows = slice(t * n, (t + 1) * n)
        carry = jnp.dot(before, every[rows].astype(BF16), preferred_element_type=F32)
        rank = rank + jnp.where(dest == t, inside[rows] + carry, 0.0)
    return dest * capacity + rank.astype(jnp.int32) - 1


def place(record_ref, slot_ref, blocks):
    total = None
    for j in range(0, slot_ref.shape[0], 2):
        slot = wide_row(slot_ref, j)
        lane = one_hot(slot & (LANES - 1), LANES)
        block = slot >> (LANES.bit_length() - 1)
        record = jnp.concatenate(
            [record_ref[pl.ds(SUB * j, SUB), :], record_ref[pl.ds(SUB * (j + 1), SUB), :]], axis=1
        )
        parts = [p.astype(F32) for p in halves(record)]
        spread = [
            jnp.concatenate(
                [jnp.where(block == b, p, 0.0) for b in range(blocks)], axis=0
            ).astype(BF16)
            for p in parts
        ]
        piece = dot_nt(jnp.concatenate(spread, axis=1), jnp.concatenate([lane, lane], axis=1))
        total = piece if total is None else total + piece
    return total


def send_records(out_ref, placed, turned):
    sectors = out_ref.shape[0]
    out_ref[:, : 2 * SUB, :] = placed.reshape(sectors, 2 * SUB, LANES)
    near = jnp.concatenate([t[:2] for t in turned] + [jnp.zeros((2, LANES), F32)], axis=0)
    for t in range(sectors):
        out_ref[t, 2 * SUB :, :] = near


def edges(planes_ref, first_z, last_z, first_a, last_a, count_z, count_a):
    for c in range(3):
        first_z[c] = planes_ref[c, :count_a, :]
        last_z[c] = planes_ref[c, (count_z - 1) * count_a :, :]
        first_a[c] = planes_ref[c, pl.ds(0, count_z, stride=count_a), :]
        last_a[c] = planes_ref[c, pl.ds(count_a - 1, count_z, stride=count_a), :]


def first_kernel(
    gas, mass, temp, speed, cell, dest, out, source, first_z, last_z, first_a, last_a, gathered, slots, records
):
    sectors = out.shape[0]
    count_a = first_z.shape[1]
    count_z = first_a.shape[1]
    table, turned = gas_table([gas[c] for c in range(3)])
    sample(table, cell, gathered)
    states = (mass[...], temp[...], speed[...])
    live = jnp.where(states[0] > 0, 1.0, 0.0)
    change, terms = droplet_rates(states, [gathered[c] for c in range(3)], live)
    n = cell.shape[0]
    records[...] = jnp.zeros(records.shape, F32)
    for c in range(3):
        source[c] = terms[c]
        records[pl.ds(c, n, stride=SUB), :] = states[c] + DT_STEP * change[c]
        records[pl.ds(3 + c, n, stride=SUB), :] = states[c]
    slots[...] = slot_of(dest[...], sectors, 2 * LANES)
    send_records(out, place(records, slots, 2 * sectors), turned)
    edges(gas, first_z, last_z, first_a, last_a, count_z, count_a)


def deposit_kernel(source, cell, out):
    total = deposit(source, cell, out.shape[1], out.shape[2])
    for c in range(3):
        out[c] = total[:, c * LANES : (c + 1) * LANES]


def stencil(gas, added, z_next, z_prev, a_next, a_prev, near, aspect, count_z, count_a):
    shape = (count_z, count_a, LANES)
    radius = iota((1, 1, LANES), 2)
    pos = radius.astype(F32) + 0.5
    inverse = 1.0 / (12.0 * pos)
    geometry = aspect * aspect / jnp.maximum(pos / LANES, RADIUS_FLOOR) ** 2
    across = jnp.concatenate([near, jnp.zeros((LANES - SUB, LANES), F32)], axis=0).T
    lane = iota(shape, 2)
    column = iota(shape, 1)
    fields = [gas[c].reshape(shape) for c in range(3)]
    results = []
    for c in range(3):
        q = fields[c]
        edge = 2.0 * WALL_VALUES[c]
        near_0 = across[:, 2 * c : 2 * c + 1].reshape(count_z, count_a, 1)
        near_1 = across[:, 2 * c + 1 : 2 * c + 2].reshape(count_z, count_a, 1)
        up = pltpu.roll(q, LANES - 1, 2)
        down = pltpu.roll(q, 1, 2)
        up_2 = pltpu.roll(q, LANES - 2, 2)
        down_2 = pltpu.roll(q, 2, 2)
        plus_one = jnp.where(lane == LANES - 1, edge - q, up)
        plus_two = jnp.where(
            lane == LANES - 1, edge - down, jnp.where(lane == LANES - 2, edge - up, up_2)
        )
        minus_one = jnp.where(lane == 0, near_0, down)
        minus_two = jnp.where(lane == 0, near_1, jnp.where(lane == 1, near_0, down_2))
        following = jnp.concatenate([q[1:], z_next[c].reshape(1, count_a, LANES)], axis=0)
        preceding = jnp.concatenate([z_prev[c].reshape(1, count_a, LANES), q[:-1]], axis=0)
        right = jnp.where(
            column == count_a - 1,
            a_next[c].reshape(count_z, 1, LANES),
            pltpu.roll(q, count_a - 1, 1),
        )
        left = jnp.where(column == 0, a_prev[c].reshape(count_z, 1, LANES), pltpu.roll(q, 1, 1))
        laplace = (16.0 * (plus_one + minus_one) - 30.0 * q - plus_two - minus_two) / 12.0
        laplace = laplace + (8.0 * (plus_one - minus_one) - plus_two + minus_two) * inverse
        laplace = laplace + geometry * (right + left - 2.0 * q)
        laplace = laplace + (following + preceding - 2.0 * q) / 16.0
        results.append(
            q
            + DIFFUSION[c] * laplace
            - ADVECT * fields[2] * (following - preceding)
            + DT_STEP * (added[c].reshape(shape) + FORCING[c])
        )
    return results


def middle_kernel(
    aspect, gas, added, z_next, z_prev, a_next, a_prev, arrived, partner, cell, dest,
    middle, near_out, gathered, slots, first_z, last_z, first_a, last_a,
):
    count_a = z_next.shape[1]
    count_z = a_next.shape[1]
    near = arrived[partner[0], 2 * SUB :, :]
    results = stencil(gas, added, z_next, z_prev, a_next, a_prev, near, aspect, count_z, count_a)
    for c in range(3):
        middle[c] = results[c].reshape(middle.shape[1:])
    table, turned = gas_table([middle[c] for c in range(3)])
    near_out[...] = jnp.concatenate([t[:2] for t in turned] + [jnp.zeros((2, LANES), F32)], axis=0)
    sample(table, cell, gathered)
    slots[...] = slot_of(dest[...], arrived.shape[0], 2 * LANES)
    edges(middle, first_z, last_z, first_a, last_a, count_z, count_a)


def second_kernel(arrived, near, gathered, slots, out, source, records):
    sectors = arrived.shape[0]
    n = gathered.shape[1]
    for half in range(2):
        fields = [arrived[:, half * SUB + c, :] for c in range(6)]
        now, anchor = fields[:3], fields[3:]
        live = jnp.where(anchor[0] > 0, 1.0, 0.0)
        rows = pl.ds(half, sectors, stride=2)
        change, terms = droplet_rates(now, [gathered[c, rows, :] for c in range(3)], live)
        for c in range(3):
            source[c, rows, :] = terms[c]
            final = 0.75 * anchor[c] + 0.25 * (now[c] + DT_STEP * change[c])
            records[pl.ds(half * SUB + c, sectors, stride=2 * SUB), :] = final
            records[pl.ds(half * SUB + 3 + c, sectors, stride=2 * SUB), :] = anchor[c]
        for c in range(6, SUB):
            records[pl.ds(half * SUB + c, sectors, stride=2 * SUB), :] = jnp.zeros((sectors, LANES), F32)
    placed = place(records, slots, 2 * sectors)
    out[:, : 2 * SUB, :] = placed.reshape(sectors, 2 * SUB, LANES)
    for t in range(sectors):
        out[t, 2 * SUB :, :] = near[...]


def last_kernel(aspect, gas, middle, added, z_next, z_prev, a_next, a_prev, arrived, partner, out, records):
    count_a = z_next.shape[1]
    count_z = a_next.shape[1]
    near = arrived[partner[0], 2 * SUB :, :]
    results = stencil(middle, added, z_next, z_prev, a_next, a_prev, near, aspect, count_z, count_a)
    for c in range(3):
        out[c] = 0.75 * gas[c] + 0.25 * results[c].reshape(out.shape[1:])
    for s in range(arrived.shape[0]):
        for half in range(2):
            at = (2 * s + half) * LANES
            records[:, at : at + LANES] = arrived[s, half * SUB : half * SUB + 6, :]


def kernel(body, outs, scratch=(), smem=(), n_in=0):
    def spec(i):
        return pl.BlockSpec(memory_space=pltpu.SMEM if i in smem else pltpu.VMEM)

    return pl.pallas_call(
        body,
        out_shape=[jax.ShapeDtypeStruct(s, d) for s, d in outs],
        in_specs=[spec(i) for i in range(n_in)],
        out_specs=[pl.BlockSpec(memory_space=pltpu.VMEM) for _ in outs],
        scratch_shapes=list(scratch),
        compiler_params=pltpu.CompilerParams(vmem_limit_bytes=VMEM_LIMIT),
    )


def shifts(first, last, axis):
    count = lax.axis_size(axis)
    ahead = [((i + 1) % count, i) for i in range(count)]
    behind = [(i, (i + 1) % count) for i in range(count)]
    return lax.ppermute(first, axis, ahead), lax.ppermute(last, axis, behind)


def body(gas_fields, drop_mass, drop_temp, drop_speed, dest_first, cell_first, dest_second, cell_second):
    sectors = lax.axis_size("azim")
    _, count_z, count_a, radial = gas_fields.shape
    aspect = count_a * sectors / (2.0 * math.pi * radial)
    cells = count_z * count_a
    n1 = drop_mass.shape[0] // LANES
    n2 = cell_second.shape[0] // LANES
    gas = gas_fields.reshape(3, cells, radial)
    block = (sectors, 3 * SUB, LANES)
    z_edge = ((3, count_a, radial), F32)
    a_edge = ((3, count_z, radial), F32)
    planes = ((3, cells, radial), F32)
    partner = (lax.axis_index("azim") ^ (sectors // 2)).astype(jnp.int32).reshape(1)

    out_1, source_1, first_z, last_z, first_a, last_a = kernel(
        first_kernel,
        [(block, F32), ((3, n1, LANES), F32), z_edge, z_edge, a_edge, a_edge],
        [pltpu.VMEM((3, n1, LANES), F32), pltpu.VMEM((n1, LANES), jnp.int32), pltpu.VMEM((n1 * SUB, LANES), F32)],
        n_in=6,
    )(
        gas,
        drop_mass.reshape(n1, LANES),
        drop_temp.reshape(n1, LANES),
        drop_speed.reshape(n1, LANES),
        cell_first.reshape(n1, LANES),
        dest_first.reshape(n1, LANES),
    )
    arrived_1 = lax.all_to_all(out_1, "azim", split_axis=0, concat_axis=0, tiled=True)
    a_next, a_prev = shifts(first_a, last_a, "azim")
    z_next, z_prev = shifts(first_z, last_z, "axial")
    (added_1,) = kernel(deposit_kernel, [planes], n_in=2)(source_1, cell_first.reshape(n1, LANES))

    cell_2 = cell_second.reshape(n2, LANES)
    middle, near_2, gathered_2, slots_2, first_z, last_z, first_a, last_a = kernel(
        lambda *refs: middle_kernel(aspect, *refs),
        [planes, ((SUB, LANES), F32), ((3, n2, LANES), F32), ((n2, LANES), jnp.int32), z_edge, z_edge, a_edge, a_edge],
        smem=(7,),
        n_in=10,
    )(gas, added_1, z_next, z_prev, a_next, a_prev, arrived_1, partner, cell_2, dest_second.reshape(n2, LANES))
    a_next, a_prev = shifts(first_a, last_a, "azim")
    z_next, z_prev = shifts(first_z, last_z, "axial")

    out_2, source_2 = kernel(
        second_kernel,
        [(block, F32), ((3, n2, LANES), F32)],
        [pltpu.VMEM((n2 * SUB, LANES), F32)],
        n_in=4,
    )(arrived_1, near_2, gathered_2, slots_2)
    arrived_2 = lax.all_to_all(out_2, "azim", split_axis=0, concat_axis=0, tiled=True)
    (added_2,) = kernel(deposit_kernel, [planes], n_in=2)(source_2, cell_2)
    gas_next, drop_records = kernel(
        lambda *refs: last_kernel(aspect, *refs),
        [planes, ((6, n2 * LANES), F32)],
        smem=(8,),
        n_in=9,
    )(gas, middle, added_2, z_next, z_prev, a_next, a_prev, arrived_2, partner)
    return gas_next.reshape(gas_fields.shape), drop_records


def solution(mesh):
    rows = P(("axial", "azim"))
    columns = P(("axial", "azim"), None)
    placed = (P(None, "axial", "azim", None), rows, rows, rows, columns, rows, columns, rows)
    return jax.shard_map(
        body,
        mesh=mesh,
        in_specs=placed,
        out_specs=(P(None, "axial", "azim", None), P(None, ("axial", "azim"))),
        check_vma=False,
    )
```

```python
import math

import jax
import jax.numpy as jnp
from jax import lax
from jax.experimental import pallas as pl
from jax.experimental.pallas import tpu as pltpu
from jax.sharding import PartitionSpec as P

DT_STEP = 0.01
TAU_HEAT = 0.04
TAU_MASS = 0.05
TAU_DRAG = 0.03
LATENT = 0.5
COUPLING = 1.0
FORCING = (0.0, 0.0, 4.0)
ADVECT = 0.16
RADIUS_FLOOR = 0.7
DIFFUSION = (0.2, 0.15, 0.17)
WALL_VALUES = (1.0, 0.0, 0.0)

F32 = jnp.float32
BF16 = jnp.bfloat16
LANES = 128
SUB = 8
VMEM_LIMIT = 40 << 20
WHOLE_VMEM = 60 << 20
COST_SCALE = 1.0


def iota(shape, dim):
    return lax.broadcasted_iota(jnp.int32, shape, dim)


def one_hot(row, size):
    hit = iota((size, row.shape[1]), 0) == row
    return jnp.where(hit, 1.0, 0.0).astype(BF16)


def halves(x):
    head = x.astype(BF16)
    return head, (x - head.astype(F32)).astype(BF16)


def wide_row(ref, j):
    return jnp.concatenate([ref[pl.ds(j, 1), :], ref[pl.ds(j + 1, 1), :]], axis=1)


def dot_nt(a, b):
    return lax.dot_general(a, b, (((1,), (1,)), ((), ())), preferred_element_type=F32)


def gas_table(planes):
    turned = [p.T for p in planes]
    parts = [jnp.concatenate(halves(t), axis=1) for t in turned]
    return jnp.concatenate(parts, axis=0), turned


def sample(table, cell_ref, out_ref):
    size = table.shape[1] // 2
    lanes_r = table.shape[0] // 3
    shift = lanes_r.bit_length() - 1
    for j in range(0, cell_ref.shape[0], 2):
        cell = wide_row(cell_ref, j)
        pick = one_hot(cell >> shift, size)
        mixed = jnp.dot(table, jnp.concatenate([pick, pick], axis=0), preferred_element_type=F32)
        here = iota((lanes_r, cell.shape[1]), 0) == (cell & (lanes_r - 1))
        for c in range(3):
            part = jnp.where(here, mixed[c * lanes_r : (c + 1) * lanes_r], 0.0)
            row = jnp.sum(part, axis=0, keepdims=True)
            out_ref[c, pl.ds(j, 1), :] = row[:, :LANES]
            out_ref[c, pl.ds(j + 1, 1), :] = row[:, LANES:]


def droplet_rates(states, gas, live):
    mass, temp, speed = states
    excess = 0.3 + 0.2 * jnp.tanh(temp) - gas[1]
    evaporate = mass * excess / TAU_MASS
    heating = gas[0] - temp
    drag = gas[2] - speed
    change = (
        -evaporate * live,
        (heating / TAU_HEAT - LATENT * excess / TAU_MASS) * live,
        drag / TAU_DRAG * live,
    )
    source = (
        -COUPLING * mass * heating / TAU_HEAT,
        COUPLING * evaporate,
        -COUPLING * mass * drag / TAU_DRAG,
    )
    return change, source


def deposit(source_ref, cell_ref, rows, lanes_r):
    shift = lanes_r.bit_length() - 1
    low = lanes_r // 2
    total = None
    for j in range(0, cell_ref.shape[0], 2):
        cell = wide_row(cell_ref, j)
        column = jnp.where((cell & low) > 0, rows, 0) + (cell >> shift)
        here = iota((low, cell.shape[1]), 0) == (cell & (low - 1))
        pairs = [halves(wide_row(source_ref.at[c], j)) for c in range(3)]
        spread = [
            jnp.where(here, pairs[c][part].astype(F32), 0.0) for part in range(2) for c in range(3)
        ]
        piece = dot_nt(jnp.concatenate(spread, axis=0).astype(BF16), one_hot(column, 2 * rows))
        total = piece if total is None else total + piece
    total = total[: 3 * low] + total[3 * low :]
    planes = [total[c * low : (c + 1) * low] for c in range(3)]
    return [jnp.concatenate([p[:, :rows], p[:, rows:]], axis=0).T for p in planes]


def slot_of(dest, sectors, capacity):
    n = dest.shape[0]
    hits = jnp.concatenate(
        [jnp.where(dest == t, 1.0, 0.0) for t in range(sectors)], axis=0
    ).astype(BF16)
    upto = jnp.where(iota((LANES, LANES), 0) <= iota((LANES, LANES), 1), 1.0, 0.0).astype(BF16)
    inside = jnp.dot(hits, upto, preferred_element_type=F32)
    every = jnp.dot(hits, jnp.ones((LANES, LANES), BF16), preferred_element_type=F32)
    before = jnp.where(iota((n, n), 1) < iota((n, n), 0), 1.0, 0.0).astype(BF16)
    rank = jnp.zeros(dest.shape, F32)
    for t in range(sectors):
        rows = slice(t * n, (t + 1) * n)
        carry = jnp.dot(before, every[rows].astype(BF16), preferred_element_type=F32)
        rank = rank + jnp.where(dest == t, inside[rows] + carry, 0.0)
    return dest * capacity + rank.astype(jnp.int32) - 1


def place(record_ref, slot_ref, out_ref):
    sectors = out_ref.shape[0]
    capacity = 2 * LANES
    total = None
    for j in range(0, slot_ref.shape[0], 2):
        slot = wide_row(slot_ref, j)
        sector = slot >> (capacity.bit_length() - 1)
        record = jnp.concatenate(
            [record_ref[pl.ds(SUB * j, SUB), :], record_ref[pl.ds(SUB * (j + 1), SUB), :]], axis=1
        )
        spread = [
            jnp.where(sector == t, part.astype(F32), 0.0)
            for part in halves(record)
            for t in range(sectors)
        ]
        piece = dot_nt(
            jnp.concatenate(spread, axis=0).astype(BF16), one_hot(slot & (capacity - 1), capacity)
        )
        total = piece if total is None else total + piece
    count = sectors * SUB
    total = total[:count] + total[count:]
    out_ref[:, :SUB, :] = total[:, :LANES].reshape(sectors, SUB, LANES)
    out_ref[:, SUB : 2 * SUB, :] = total[:, LANES:].reshape(sectors, SUB, LANES)


def near_rows(turned):
    return jnp.concatenate([t[:2] for t in turned] + [jnp.zeros((2, LANES), F32)], axis=0)


def send_near(out_ref, near):
    for t in range(out_ref.shape[0]):
        out_ref[t, 2 * SUB :, :] = near


def columns_of(ref, c, at, count_z, count_a):
    return ref[c, pl.ds(at, count_z, stride=count_a), :]


def first_kernel(
    gas_hbm, mass_hbm, temp_hbm, speed_hbm, cell_hbm, dest_hbm,
    out, source, first_a, last_a,
    gas, mass, temp, speed, cell, dest, sems, gathered, slots, records,
):
    sectors = out.shape[0]
    count_z = first_a.shape[1]
    count_a = gas.shape[1] // count_z
    loads = [
        pltpu.make_async_copy(a, b, sems.at[i])
        for i, (a, b) in enumerate(
            (
                (dest_hbm, dest),
                (gas_hbm, gas),
                (cell_hbm, cell),
                (mass_hbm, mass),
                (temp_hbm, temp),
                (speed_hbm, speed),
            )
        )
    ]
    for load in loads:
        load.start()
    records[...] = jnp.zeros(records.shape, F32)
    loads[0].wait()
    slots[...] = slot_of(dest[...], sectors, 2 * LANES)
    for load in loads[1:]:
        load.wait()
    table, turned = gas_table([gas[c] for c in range(3)])
    send_near(out, near_rows(turned))
    sample(table, cell, gathered)
    states = (mass[...], temp[...], speed[...])
    live = jnp.where(states[0] > 0, 1.0, 0.0)
    change, terms = droplet_rates(states, [gathered[c] for c in range(3)], live)
    n = cell.shape[0]
    for c in range(3):
        source[c] = terms[c]
        records[pl.ds(c, n, stride=SUB), :] = states[c] + DT_STEP * change[c]
        records[pl.ds(3 + c, n, stride=SUB), :] = states[c]
    place(records, slots, out)
    for c in range(3):
        first_a[c] = columns_of(gas, c, 0, count_z, count_a)
        last_a[c] = columns_of(gas, c, count_a - 1, count_z, count_a)


def first_deposit_kernel(sectors, count_a, source, cell, gas, dest, out, far_z, near_z, slots):
    total = deposit(source, cell, out.shape[1], out.shape[2])
    end = out.shape[1]
    even = (lax.axis_index("axial") & 1) == 0
    for c in range(3):
        out[c] = total[c]
        first = [gas[c, :count_a, :], gas[c, count_a : 2 * count_a, :], total[c][:count_a]]
        last = [
            gas[c, end - count_a :, :],
            gas[c, end - 2 * count_a : end - count_a, :],
            total[c][end - count_a :],
        ]
        for i in range(3):
            near_z[3 * c + i] = jnp.where(even, last[i], first[i])
            far_z[3 * c + i] = jnp.where(even, first[i], last[i])
    slots[...] = slot_of(dest[...], sectors, 2 * LANES)


def stencil(fields, following, preceding, right_edge, left_edge, near, added, aspect):
    shape = fields[0].shape
    count_a = shape[1]
    pos = iota((1, 1, LANES), 2).astype(F32) + 0.5
    inverse = 1.0 / (12.0 * pos)
    geometry = aspect * aspect / jnp.maximum(pos / LANES, RADIUS_FLOOR) ** 2
    lane = iota(shape, 2)
    column = iota(shape, 1)
    results = []
    for c in range(3):
        q = fields[c]
        edge = 2.0 * WALL_VALUES[c]
        near_0, near_1 = near[c]
        up = pltpu.roll(q, LANES - 1, 2)
        down = pltpu.roll(q, 1, 2)
        up_2 = pltpu.roll(q, LANES - 2, 2)
        down_2 = pltpu.roll(q, 2, 2)
        plus_one = jnp.where(lane == LANES - 1, edge - q, up)
        plus_two = jnp.where(
            lane == LANES - 1, edge - down, jnp.where(lane == LANES - 2, edge - up, up_2)
        )
        minus_one = jnp.where(lane == 0, near_0, down)
        minus_two = jnp.where(lane == 0, near_1, jnp.where(lane == 1, near_0, down_2))
        right = jnp.where(column == count_a - 1, right_edge[c], pltpu.roll(q, count_a - 1, 1))
        left = jnp.where(column == 0, left_edge[c], pltpu.roll(q, 1, 1))
        laplace = (16.0 * (plus_one + minus_one) - 30.0 * q - plus_two - minus_two) / 12.0
        laplace = laplace + (8.0 * (plus_one - minus_one) - plus_two + minus_two) * inverse
        laplace = laplace + geometry * (right + left - 2.0 * q)
        laplace = laplace + (following[c] + preceding[c] - 2.0 * q) / 16.0
        results.append(
            q
            + DIFFUSION[c] * laplace
            - ADVECT * fields[2] * (following[c] - preceding[c])
            + DT_STEP * (added[c] + FORCING[c])
        )
    return results


def between(q, z_prev, z_next):
    return (
        jnp.concatenate([q[1:], z_next[None]], axis=0),
        jnp.concatenate([z_prev[None], q[:-1]], axis=0),
    )


def near_columns(near):
    return jnp.concatenate([near, jnp.zeros((LANES - SUB, LANES), F32)], axis=0).T


def column_blocks(across, count_z, count_a):
    return [
        [across[:, 2 * c + i : 2 * c + i + 1].reshape(count_z, count_a, 1) for i in range(2)]
        for c in range(3)
    ]


def across_axis(sectors):
    return lax.axis_index("azim") ^ (sectors // 2)


def outer_planes(near_z, far_z):
    even = (lax.axis_index("axial") & 1) == 0
    count = range(near_z.shape[0])
    return (
        [jnp.where(even, near_z[i], far_z[i]) for i in count],
        [jnp.where(even, far_z[i], near_z[i]) for i in count],
    )


def middle_kernel(
    aspect, gas, added, far_z, near_z, a_next, a_prev, arrived,
    middle, near, first_a, last_a,
):
    count_z, count_a = a_next.shape[1], near_z.shape[1]
    shape = (count_z, count_a, LANES)
    z_next, z_prev = outer_planes(near_z, far_z)
    across = near_columns(arrived[across_axis(arrived.shape[0]), 2 * SUB :, :])
    fields = [gas[c].reshape(shape) for c in range(3)]
    pairs = [between(fields[c], z_prev[3 * c], z_next[3 * c]) for c in range(3)]
    results = stencil(
        fields,
        [p[0] for p in pairs],
        [p[1] for p in pairs],
        [a_next[c].reshape(count_z, 1, LANES) for c in range(3)],
        [a_prev[c].reshape(count_z, 1, LANES) for c in range(3)],
        column_blocks(across, count_z, count_a),
        [added[c].reshape(shape) for c in range(3)],
        aspect,
    )
    for c in range(3):
        middle[c] = results[c].reshape(middle.shape[1:])
    outer = [planes[3 * c] for c in range(3) for planes in (z_prev, z_next)]
    for i, plane in enumerate(outer):
        first_a[3 * count_z + i] = plane[0]
        last_a[3 * count_z + i] = plane[count_a - 1]
    for c in range(3):
        first_a[c * count_z : (c + 1) * count_z] = columns_of(middle, c, 0, count_z, count_a)
        last_a[c * count_z : (c + 1) * count_z] = columns_of(middle, c, count_a - 1, count_z, count_a)
    unused = first_a.shape[0] - 3 * count_z - len(outer)
    first_a[3 * count_z + len(outer) :] = jnp.zeros((unused, LANES), F32)
    last_a[3 * count_z + len(outer) :] = jnp.zeros((unused, LANES), F32)
    rest = jnp.zeros((LANES - len(outer) * count_a, LANES), F32)
    near[...] = jnp.concatenate(outer + [rest], axis=0).T[:2]


def sample_kernel(middle, outer_near, cell, gathered, near):
    table, turned = gas_table([middle[c] for c in range(3)])
    sample(table, cell, gathered)
    near[...] = jnp.concatenate([t[:2] for t in turned] + [outer_near[...]], axis=0)


def second_kernel(gathered, near, arrived, slots, a_next, a_prev, out, source, records):
    del a_next, a_prev
    send_near(out, near[...])
    sectors = arrived.shape[0]
    for half in range(2):
        values = [arrived[:, half * SUB + c, :] for c in range(6)]
        now, anchor = values[:3], values[3:]
        live = jnp.where(anchor[0] > 0, 1.0, 0.0)
        rows = pl.ds(half, sectors, stride=2)
        change, terms = droplet_rates(now, [gathered[c, rows, :] for c in range(3)], live)
        for c in range(3):
            source[c, rows, :] = terms[c]
            final = 0.75 * anchor[c] + 0.25 * (now[c] + DT_STEP * change[c])
            records[pl.ds(half * SUB + c, sectors, stride=2 * SUB), :] = final
            records[pl.ds(half * SUB + 3 + c, sectors, stride=2 * SUB), :] = anchor[c]
        for c in range(6, SUB):
            records[pl.ds(half * SUB + c, sectors, stride=2 * SUB), :] = jnp.zeros((sectors, LANES), F32)
    place(records, slots, out)


def last_kernel(aspect, gas, middle, source, cell, far_z, near_z, a_next, a_prev, arrived, out, records):
    added = deposit(source, cell, gas.shape[1], gas.shape[2])
    count_a = near_z.shape[1]
    z_next, z_prev = outer_planes(near_z, far_z)
    count_z = gas.shape[1] // count_a
    shape = (count_z, count_a, LANES)
    end = gas.shape[1]
    across = near_columns(arrived[across_axis(arrived.shape[0]), 2 * SUB :, :])
    own = count_z * 3

    def outer(before, after):
        return jnp.concatenate([before[None], after[None]], axis=0)

    def outer_rows(ref, c):
        return ref[own + 2 * c : own + 2 * c + 2, :].reshape(2, 1, LANES)

    halo = stencil(
        [outer(z_prev[3 * c], z_next[3 * c]) for c in range(3)],
        [outer(gas[c, :count_a, :], z_next[3 * c + 1]) for c in range(3)],
        [outer(z_prev[3 * c + 1], gas[c, end - count_a :, :]) for c in range(3)],
        [outer_rows(a_next, c) for c in range(3)],
        [outer_rows(a_prev, c) for c in range(3)],
        [
            [
                across[2 * c * count_a : 2 * (c + 1) * count_a, 6 + i : 7 + i].reshape(2, count_a, 1)
                for i in range(2)
            ]
            for c in range(3)
        ],
        [outer(z_prev[3 * c + 2], z_next[3 * c + 2]) for c in range(3)],
        aspect,
    )
    fields = [middle[c].reshape(shape) for c in range(3)]
    pairs = [between(fields[c], halo[c][0], halo[c][1]) for c in range(3)]
    results = stencil(
        fields,
        [p[0] for p in pairs],
        [p[1] for p in pairs],
        [a_next[c * count_z : (c + 1) * count_z, :].reshape(count_z, 1, LANES) for c in range(3)],
        [a_prev[c * count_z : (c + 1) * count_z, :].reshape(count_z, 1, LANES) for c in range(3)],
        column_blocks(across, count_z, count_a),
        [added[c].reshape(shape) for c in range(3)],
        aspect,
    )
    for c in range(3):
        out[c] = 0.75 * gas[c] + 0.25 * results[c].reshape(out.shape[1:])
    for s in range(arrived.shape[0]):
        for half in range(2):
            at = (2 * s + half) * LANES
            records[:, at : at + LANES] = arrived[s, half * SUB : half * SUB + 6, :]


def kernel(body, outs, scratch=(), smem=(), n_in=0, home=pltpu.VMEM, limit=VMEM_LIMIT, cost=1.0):
    def spec(i):
        return pl.BlockSpec(memory_space=pltpu.SMEM if i in smem else home)

    return pl.pallas_call(
        body,
        out_shape=[jax.ShapeDtypeStruct(s, d) for s, d in outs],
        in_specs=[spec(i) for i in range(n_in)],
        out_specs=[pl.BlockSpec(memory_space=pltpu.VMEM) for _ in outs],
        scratch_shapes=list(scratch),
        compiler_params=pltpu.CompilerParams(vmem_limit_bytes=limit),
        cost_estimate=pl.CostEstimate(flops=int(cost * 1e9 * COST_SCALE), bytes_accessed=0, transcendentals=0),
    )


def shifts(first, last, axis):
    count = lax.axis_size(axis)
    ahead = [((i + 1) % count, i) for i in range(count)]
    behind = [(i, (i + 1) % count) for i in range(count)]
    return lax.ppermute(first, axis, ahead), lax.ppermute(last, axis, behind)


def swaps(near, far, axis):
    count = lax.axis_size(axis)
    odd = [(i, (i + (1 if i % 2 else -1)) % count) for i in range(count)]
    even = [(i, i ^ 1) for i in range(count)]
    near = lax.ppermute(near, axis, even)
    return lax.ppermute(far, axis, odd), near


def body(gas_fields, drop_mass, drop_temp, drop_speed, dest_first, cell_first, dest_second, cell_second):
    sectors = lax.axis_size("azim")
    _, count_z, count_a, radial = gas_fields.shape
    aspect = count_a * sectors / (2.0 * math.pi * radial)
    cells = count_z * count_a
    n1 = drop_mass.shape[0] // LANES
    n2 = cell_second.shape[0] // LANES
    gas = gas_fields.reshape(3, cells, radial)
    block = (sectors, 3 * SUB, LANES)
    z_edge = ((9, count_a, radial), F32)
    a_edge = ((3, count_z, radial), F32)
    a_edge_2 = ((-(-(3 * count_z + 6) // SUB) * SUB, radial), F32)
    planes = ((3, cells, radial), F32)
    cell_1 = cell_first.reshape(n1, LANES)
    cell_2 = cell_second.reshape(n2, LANES)

    out_1, source_1, first_a, last_a = kernel(
        first_kernel,
        [(block, F32), ((3, n1, LANES), F32), a_edge, a_edge],
        [pltpu.VMEM((3, cells, radial), F32)]
        + [pltpu.VMEM((n1, LANES), F32)] * 3
        + [pltpu.VMEM((n1, LANES), jnp.int32)] * 2
        + [pltpu.SemaphoreType.DMA((6,))]
        + [pltpu.VMEM((3, n1, LANES), F32), pltpu.VMEM((n1, LANES), jnp.int32), pltpu.VMEM((n1 * SUB, LANES), F32)],
        n_in=6,
        home=pltpu.HBM,
        limit=WHOLE_VMEM,
        cost=3.0,
    )(
        gas,
        drop_mass.reshape(n1, LANES),
        drop_temp.reshape(n1, LANES),
        drop_speed.reshape(n1, LANES),
        cell_1,
        dest_first.reshape(n1, LANES),
    )
    arrived_1 = lax.all_to_all(out_1, "azim", split_axis=0, concat_axis=0, tiled=True)
    a_next, a_prev = shifts(first_a, last_a, "azim")
    added_1, far_z, near_z, slots_2 = kernel(
        lambda *refs: first_deposit_kernel(sectors, count_a, *refs),
        [planes, z_edge, z_edge, ((n2, LANES), jnp.int32)],
        n_in=4,
        cost=1.4,
    )(source_1, cell_1, gas, dest_second.reshape(n2, LANES))
    far_z, near_z = swaps(near_z, far_z, "axial")

    middle, outer_near, first_a, last_a = kernel(
        lambda *refs: middle_kernel(aspect, *refs),
        [planes, ((2, LANES), F32), a_edge_2, a_edge_2],
        n_in=7,
    )(gas, added_1, far_z, near_z, a_next, a_prev, arrived_1)
    a_next, a_prev = shifts(first_a, last_a, "azim")
    gathered_2, near_2 = kernel(
        sample_kernel, [((3, n2, LANES), F32), ((SUB, LANES), F32)], n_in=3, cost=1.2
    )(middle, outer_near, cell_2)
    out_2, source_2 = kernel(
        second_kernel,
        [(block, F32), ((3, n2, LANES), F32)],
        [pltpu.VMEM((n2 * SUB, LANES), F32)],
        n_in=6,
        cost=2.4,
    )(gathered_2, near_2, arrived_1, slots_2, a_next, a_prev)
    arrived_2 = lax.all_to_all(out_2, "azim", split_axis=0, concat_axis=0, tiled=True)
    gas_next, drop_records = kernel(
        lambda *refs: last_kernel(aspect, *refs),
        [planes, ((6, n2 * LANES), F32)],
        n_in=9,
        cost=1.8,
    )(gas, middle, source_2, cell_2, far_z, near_z, a_next, a_prev, arrived_2)
    return gas_next.reshape(gas_fields.shape), drop_records


def solution(mesh):
    rows = P(("axial", "azim"))
    columns = P(("axial", "azim"), None)
    placed = (P(None, "axial", "azim", None), rows, rows, rows, columns, rows, columns, rows)
    return jax.shard_map(
        body,
        mesh=mesh,
        in_specs=placed,
        out_specs=(P(None, "axial", "azim", None), P(None, ("axial", "azim"))),
        check_vma=False,
    )
```

```python
import math

import jax
import jax.numpy as jnp
from jax import lax
from jax.experimental import pallas as pl
from jax.experimental.pallas import tpu as pltpu
from jax.sharding import PartitionSpec as P

DT_STEP = 0.01
TAU_HEAT = 0.04
TAU_MASS = 0.05
TAU_DRAG = 0.03
LATENT = 0.5
COUPLING = 1.0
FORCING = (0.0, 0.0, 4.0)
ADVECT = 0.16
RADIUS_FLOOR = 0.7
DIFFUSION = (0.2, 0.15, 0.17)
WALL_VALUES = (1.0, 0.0, 0.0)

F32 = jnp.float32
BF16 = jnp.bfloat16
LANES = 128
SUB = 8
VMEM_LIMIT = 40 << 20
WHOLE_VMEM = 60 << 20
COST_SCALE = 1.0


def iota(shape, dim):
    return lax.broadcasted_iota(jnp.int32, shape, dim)


def one_hot(row, size):
    hit = iota((size, row.shape[1]), 0) == row
    return jnp.where(hit, 1.0, 0.0).astype(BF16)


def halves(x):
    head = x.astype(BF16)
    return head, (x - head.astype(F32)).astype(BF16)


def wide_row(ref, j):
    return jnp.concatenate([ref[pl.ds(j, 1), :], ref[pl.ds(j + 1, 1), :]], axis=1)


def dot_nt(a, b):
    return lax.dot_general(a, b, (((1,), (1,)), ((), ())), preferred_element_type=F32)


def gas_table(planes):
    turned = [p.T for p in planes]
    parts = [jnp.concatenate(halves(t), axis=1) for t in turned]
    return jnp.concatenate(parts, axis=0), turned


def sample(table, cell_ref, out_ref):
    size = table.shape[1] // 2
    lanes_r = table.shape[0] // 3
    shift = lanes_r.bit_length() - 1
    for j in range(0, cell_ref.shape[0], 2):
        cell = wide_row(cell_ref, j)
        pick = one_hot(cell >> shift, size)
        mixed = jnp.dot(table, jnp.concatenate([pick, pick], axis=0), preferred_element_type=F32)
        here = iota((lanes_r, cell.shape[1]), 0) == (cell & (lanes_r - 1))
        for c in range(3):
            part = jnp.where(here, mixed[c * lanes_r : (c + 1) * lanes_r], 0.0)
            row = jnp.sum(part, axis=0, keepdims=True)
            out_ref[c, pl.ds(j, 1), :] = row[:, :LANES]
            out_ref[c, pl.ds(j + 1, 1), :] = row[:, LANES:]


def droplet_rates(states, gas, live):
    mass, temp, speed = states
    excess = 0.3 + 0.2 * jnp.tanh(temp) - gas[1]
    evaporate = mass * excess / TAU_MASS
    heating = gas[0] - temp
    drag = gas[2] - speed
    change = (
        -evaporate * live,
        (heating / TAU_HEAT - LATENT * excess / TAU_MASS) * live,
        drag / TAU_DRAG * live,
    )
    source = (
        -COUPLING * mass * heating / TAU_HEAT,
        COUPLING * evaporate,
        -COUPLING * mass * drag / TAU_DRAG,
    )
    return change, source


def deposit(source_ref, cell_ref, rows, lanes_r):
    shift = lanes_r.bit_length() - 1
    low = lanes_r // 2
    total = None
    for j in range(0, cell_ref.shape[0], 2):
        cell = wide_row(cell_ref, j)
        column = jnp.where((cell & low) > 0, rows, 0) + (cell >> shift)
        here = iota((low, cell.shape[1]), 0) == (cell & (low - 1))
        pairs = [halves(wide_row(source_ref.at[c], j)) for c in range(3)]
        spread = [
            jnp.where(here, pairs[c][part].astype(F32), 0.0) for part in range(2) for c in range(3)
        ]
        piece = dot_nt(jnp.concatenate(spread, axis=0).astype(BF16), one_hot(column, 2 * rows))
        total = piece if total is None else total + piece
    total = total[: 3 * low] + total[3 * low :]
    planes = [total[c * low : (c + 1) * low] for c in range(3)]
    return [jnp.concatenate([p[:, :rows], p[:, rows:]], axis=0).T for p in planes]


def slot_of(dest, sectors, capacity):
    n = dest.shape[0]
    hits = jnp.concatenate(
        [jnp.where(dest == t, 1.0, 0.0) for t in range(sectors)], axis=0
    ).astype(BF16)
    upto = jnp.where(iota((LANES, LANES), 0) <= iota((LANES, LANES), 1), 1.0, 0.0).astype(BF16)
    inside = jnp.dot(hits, upto, preferred_element_type=F32)
    every = jnp.dot(hits, jnp.ones((LANES, LANES), BF16), preferred_element_type=F32)
    before = jnp.where(iota((n, n), 1) < iota((n, n), 0), 1.0, 0.0).astype(BF16)
    rank = jnp.zeros(dest.shape, F32)
    for t in range(sectors):
        rows = slice(t * n, (t + 1) * n)
        carry = jnp.dot(before, every[rows].astype(BF16), preferred_element_type=F32)
        rank = rank + jnp.where(dest == t, inside[rows] + carry, 0.0)
    return dest * capacity + rank.astype(jnp.int32) - 1


def place(record_ref, slot_ref, out_ref):
    sectors = out_ref.shape[0]
    capacity = 2 * LANES
    total = None
    for j in range(0, slot_ref.shape[0], 2):
        slot = wide_row(slot_ref, j)
        sector = slot >> (capacity.bit_length() - 1)
        record = jnp.concatenate(
            [record_ref[pl.ds(SUB * j, SUB), :], record_ref[pl.ds(SUB * (j + 1), SUB), :]], axis=1
        )
        spread = [
            jnp.where(sector == t, part.astype(F32), 0.0)
            for part in halves(record)
            for t in range(sectors)
        ]
        piece = dot_nt(
            jnp.concatenate(spread, axis=0).astype(BF16), one_hot(slot & (capacity - 1), capacity)
        )
        total = piece if total is None else total + piece
    count = sectors * SUB
    total = total[:count] + total[count:]
    out_ref[:, :SUB, :] = total[:, :LANES].reshape(sectors, SUB, LANES)
    out_ref[:, SUB : 2 * SUB, :] = total[:, LANES:].reshape(sectors, SUB, LANES)


def near_rows(turned):
    return jnp.concatenate([t[:2] for t in turned] + [jnp.zeros((2, LANES), F32)], axis=0)


def send_near(out_ref, near):
    for t in range(out_ref.shape[0]):
        out_ref[t, 2 * SUB : 3 * SUB, :] = near


def columns_of(ref, c, at, count_z, count_a):
    return ref[c, pl.ds(at, count_z, stride=count_a), :]


def first_kernel(
    gas_hbm, mass_hbm, temp_hbm, speed_hbm, cell_hbm, dest_hbm,
    out, source,
    gas, mass, temp, speed, cell, dest, sems, gathered, slots, records,
):
    sectors = out.shape[0]
    loads = [
        pltpu.make_async_copy(a, b, sems.at[i])
        for i, (a, b) in enumerate(
            (
                (dest_hbm, dest),
                (gas_hbm, gas),
                (cell_hbm, cell),
                (mass_hbm, mass),
                (temp_hbm, temp),
                (speed_hbm, speed),
            )
        )
    ]
    for load in loads:
        load.start()
    records[...] = jnp.zeros(records.shape, F32)
    loads[0].wait()
    slots[...] = slot_of(dest[...], sectors, 2 * LANES)
    for load in loads[1:]:
        load.wait()
    table, turned = gas_table([gas[c] for c in range(3)])
    send_near(out, near_rows(turned))
    sample(table, cell, gathered)
    states = (mass[...], temp[...], speed[...])
    live = jnp.where(states[0] > 0, 1.0, 0.0)
    change, terms = droplet_rates(states, [gathered[c] for c in range(3)], live)
    n = cell.shape[0]
    for c in range(3):
        source[c] = terms[c]
        records[pl.ds(c, n, stride=SUB), :] = states[c] + DT_STEP * change[c]
        records[pl.ds(3 + c, n, stride=SUB), :] = states[c]
    place(records, slots, out)


def first_deposit_kernel(sectors, count_a, source, cell, gas, dest, out, far_z, near_z, first_a, last_a, slots):
    total = deposit(source, cell, out.shape[1], out.shape[2])
    end = out.shape[1]
    even = (lax.axis_index("axial") & 1) == 0
    for c in range(3):
        out[c] = total[c]
        first = [gas[c, :count_a, :], gas[c, count_a : 2 * count_a, :], total[c][:count_a]]
        last = [
            gas[c, end - count_a :, :],
            gas[c, end - 2 * count_a : end - count_a, :],
            total[c][end - count_a :],
        ]
        for i in range(3):
            near_z[3 * c + i] = jnp.where(even, last[i], first[i])
            far_z[3 * c + i] = jnp.where(even, first[i], last[i])
    count_z = first_a.shape[1]
    for c in range(3):
        for edge, at, inner in ((first_a, 0, 1), (last_a, count_a - 1, count_a - 2)):
            edge[3 * c] = columns_of(gas, c, at, count_z, count_a)
            edge[3 * c + 1] = columns_of(gas, c, inner, count_z, count_a)
            edge[3 * c + 2] = columns_of(out, c, at, count_z, count_a)
    slots[...] = slot_of(dest[...], sectors, 2 * LANES)


def last_deposit_kernel(source, cell, out):
    total = deposit(source, cell, out.shape[1], out.shape[2])
    for c in range(3):
        out[c] = total[c]


def stencil(fields, following, preceding, right, left, near, added, aspect):
    shape = fields[0].shape
    pos = iota((1, 1, LANES), 2).astype(F32) + 0.5
    inverse = 1.0 / (12.0 * pos)
    geometry = aspect * aspect / jnp.maximum(pos / LANES, RADIUS_FLOOR) ** 2
    lane = iota(shape, 2)
    results = []
    for c in range(3):
        q = fields[c]
        edge = 2.0 * WALL_VALUES[c]
        near_0, near_1 = near[c]
        up = pltpu.roll(q, LANES - 1, 2)
        down = pltpu.roll(q, 1, 2)
        up_2 = pltpu.roll(q, LANES - 2, 2)
        down_2 = pltpu.roll(q, 2, 2)
        plus_one = jnp.where(lane == LANES - 1, edge - q, up)
        plus_two = jnp.where(
            lane == LANES - 1, edge - down, jnp.where(lane == LANES - 2, edge - up, up_2)
        )
        minus_one = jnp.where(lane == 0, near_0, down)
        minus_two = jnp.where(lane == 0, near_1, jnp.where(lane == 1, near_0, down_2))
        laplace = (16.0 * (plus_one + minus_one) - 30.0 * q - plus_two - minus_two) / 12.0
        laplace = laplace + (8.0 * (plus_one - minus_one) - plus_two + minus_two) * inverse
        laplace = laplace + geometry * (right[c] + left[c] - 2.0 * q)
        laplace = laplace + (following[c] + preceding[c] - 2.0 * q) / 16.0
        results.append(
            q
            + DIFFUSION[c] * laplace
            - ADVECT * fields[2] * (following[c] - preceding[c])
            + DT_STEP * (added[c] + FORCING[c])
        )
    return results


def sides(fields, right_edge, left_edge):
    count_a = fields[0].shape[1]
    column = iota(fields[0].shape, 1)
    pairs = [
        (
            jnp.where(column == count_a - 1, right_edge[c], pltpu.roll(q, count_a - 1, 1)),
            jnp.where(column == 0, left_edge[c], pltpu.roll(q, 1, 1)),
        )
        for c, q in enumerate(fields)
    ]
    return [p[0] for p in pairs], [p[1] for p in pairs]


def between(q, z_prev, z_next):
    return (
        jnp.concatenate([q[1:], z_next[None]], axis=0),
        jnp.concatenate([z_prev[None], q[:-1]], axis=0),
    )


def near_columns(near):
    return jnp.concatenate([near, jnp.zeros((LANES - SUB, LANES), F32)], axis=0).T


def column_blocks(across, count_z, count_a):
    return [
        [across[:, 2 * c + i : 2 * c + i + 1].reshape(count_z, count_a, 1) for i in range(2)]
        for c in range(3)
    ]


def across_axis(sectors):
    return lax.axis_index("azim") ^ (sectors // 2)


def outer_planes(near_z, far_z):
    even = (lax.axis_index("axial") & 1) == 0
    count = range(near_z.shape[0])
    return (
        [jnp.where(even, near_z[i], far_z[i]) for i in count],
        [jnp.where(even, far_z[i], near_z[i]) for i in count],
    )


def middle_kernel(
    aspect, gas, added, far_z, near_z, a_next, a_prev, arrived, cell, slots,
    middle, out, source, gathered, records,
):
    count_z, count_a = a_next.shape[1], near_z.shape[1]
    shape = (count_z, count_a, LANES)
    sectors = arrived.shape[0]
    z_next, z_prev = outer_planes(near_z, far_z)
    across = near_columns(arrived[across_axis(sectors), 2 * SUB :, :])
    fields = [gas[c].reshape(shape) for c in range(3)]
    pairs = [between(fields[c], z_prev[3 * c], z_next[3 * c]) for c in range(3)]
    results = stencil(
        fields,
        [p[0] for p in pairs],
        [p[1] for p in pairs],
        *sides(
            fields,
            [a_next[3 * c].reshape(count_z, 1, LANES) for c in range(3)],
            [a_prev[3 * c].reshape(count_z, 1, LANES) for c in range(3)],
        ),
        column_blocks(across, count_z, count_a),
        [added[c].reshape(shape) for c in range(3)],
        aspect,
    )
    for c in range(3):
        middle[c] = results[c].reshape(middle.shape[1:])
    table, turned = gas_table([middle[c] for c in range(3)])
    sample(table, cell, gathered)

    outer = [planes[3 * c] for c in range(3) for planes in (z_prev, z_next)]
    rest = jnp.zeros((LANES - len(outer) * count_a, LANES), F32)
    outer_near = jnp.concatenate(outer + [rest], axis=0).T[:2]
    near = jnp.concatenate([t[:2] for t in turned] + [outer_near], axis=0)
    spare = jnp.zeros((SUB - len(outer), LANES), F32)
    to_right = jnp.concatenate([p[count_a - 1 :] for p in outer] + [spare], axis=0)
    to_left = jnp.concatenate([p[:1] for p in outer] + [spare], axis=0)
    right, across_to = neighbour(1, sectors), across_axis(sectors)
    for t in range(sectors):
        out[t, 2 * SUB :, :] = jnp.where(across_to == t, near, jnp.where(right == t, to_right, to_left))

    for half in range(2):
        values = [arrived[:, half * SUB + c, :] for c in range(6)]
        now, anchor = values[:3], values[3:]
        live = jnp.where(anchor[0] > 0, 1.0, 0.0)
        rows = pl.ds(half, sectors, stride=2)
        change, terms = droplet_rates(now, [gathered[c, rows, :] for c in range(3)], live)
        for c in range(3):
            source[c, rows, :] = terms[c]
            final = 0.75 * anchor[c] + 0.25 * (now[c] + DT_STEP * change[c])
            records[pl.ds(half * SUB + c, sectors, stride=2 * SUB), :] = final
            records[pl.ds(half * SUB + 3 + c, sectors, stride=2 * SUB), :] = anchor[c]
        for c in range(6, SUB):
            records[pl.ds(half * SUB + c, sectors, stride=2 * SUB), :] = jnp.zeros((sectors, LANES), F32)
    place(records, slots, out)


def neighbour(step, sectors):
    return (lax.axis_index("azim") + step + sectors) % sectors


def last_kernel(
    aspect, gas, middle, added, far_z, near_z, a_next, a_prev, earlier, arrived,
    out, records, turned_near,
):
    count_a = near_z.shape[1]
    count_z = gas.shape[1] // count_a
    sectors = arrived.shape[0]
    shape = (count_z, count_a, LANES)
    end = gas.shape[1]
    z_next, z_prev = outer_planes(near_z, far_z)
    across = near_columns(arrived[across_axis(sectors), 2 * SUB :, :])
    ahead, behind = neighbour(1, sectors), neighbour(-1, sectors)
    corner_next = arrived[ahead, 2 * SUB :, :]
    corner_prev = arrived[behind, 2 * SUB :, :]

    def both(before, after):
        return jnp.concatenate([before[None], after[None]], axis=0)

    outer = [both(z_prev[3 * c], z_next[3 * c]) for c in range(3)]
    planes = stencil(
        outer,
        [both(gas[c, :count_a, :], z_next[3 * c + 1]) for c in range(3)],
        [both(z_prev[3 * c + 1], gas[c, end - count_a :, :]) for c in range(3)],
        *sides(
            outer,
            [corner_next[2 * c : 2 * c + 2].reshape(2, 1, LANES) for c in range(3)],
            [corner_prev[2 * c : 2 * c + 2].reshape(2, 1, LANES) for c in range(3)],
        ),
        [
            [
                across[2 * c * count_a : 2 * (c + 1) * count_a, 6 + i : 7 + i].reshape(2, count_a, 1)
                for i in range(2)
            ]
            for c in range(3)
        ],
        [both(z_prev[3 * c + 2], z_next[3 * c + 2]) for c in range(3)],
        aspect,
    )
    columns = []
    for edge, corner, sector, at in (
        (a_prev, corner_prev, behind, count_a - 1),
        (a_next, corner_next, ahead, 0),
    ):
        turned_near[...] = near_columns(earlier[sector ^ (sectors // 2), 2 * SUB :, :])
        near = turned_near[pl.ds(at, count_z, stride=count_a), :]
        own = [columns_of(gas, c, count_a - 1 - at, count_z, count_a) for c in range(3)]
        inner = [edge[3 * c + 1] for c in range(3)]
        fields = [edge[3 * c] for c in range(3)]
        following = [
            jnp.concatenate([fields[c][1:], corner[2 * c + 1 : 2 * c + 2]], axis=0) for c in range(3)
        ]
        preceding = [
            jnp.concatenate([corner[2 * c : 2 * c + 1], fields[c][:-1]], axis=0) for c in range(3)
        ]
        columns.append(
            stencil(
                [f[None] for f in fields],
                [f[None] for f in following],
                [f[None] for f in preceding],
                [f[None] for f in own],
                [f[None] for f in inner],
                [[near[None, :, 2 * c + i : 2 * c + i + 1] for i in range(2)] for c in range(3)],
                [edge[3 * c + 2][None] for c in range(3)],
                aspect,
            )
        )
    left, right = columns
    fields = [middle[c].reshape(shape) for c in range(3)]
    pairs = [between(fields[c], planes[c][0], planes[c][1]) for c in range(3)]
    results = stencil(
        fields,
        [p[0] for p in pairs],
        [p[1] for p in pairs],
        *sides(
            fields,
            [right[c].reshape(count_z, 1, LANES) for c in range(3)],
            [left[c].reshape(count_z, 1, LANES) for c in range(3)],
        ),
        column_blocks(across, count_z, count_a),
        [added[c].reshape(shape) for c in range(3)],
        aspect,
    )
    for c in range(3):
        out[c] = 0.75 * gas[c] + 0.25 * results[c].reshape(out.shape[1:])
    for s in range(sectors):
        for half in range(2):
            at = (2 * s + half) * LANES
            records[:, at : at + LANES] = arrived[s, half * SUB : half * SUB + 6, :]


def kernel(body, outs, scratch=(), smem=(), n_in=0, home=pltpu.VMEM, limit=VMEM_LIMIT, cost=1.0):
    def spec(i):
        return pl.BlockSpec(memory_space=pltpu.SMEM if i in smem else home)

    return pl.pallas_call(
        body,
        out_shape=[jax.ShapeDtypeStruct(s, d) for s, d in outs],
        in_specs=[spec(i) for i in range(n_in)],
        out_specs=[pl.BlockSpec(memory_space=pltpu.VMEM) for _ in outs],
        scratch_shapes=list(scratch),
        compiler_params=pltpu.CompilerParams(vmem_limit_bytes=limit),
        cost_estimate=pl.CostEstimate(flops=int(cost * 1e9 * COST_SCALE), bytes_accessed=0, transcendentals=0),
    )


def shifts(first, last, axis):
    count = lax.axis_size(axis)
    ahead = [((i + 1) % count, i) for i in range(count)]
    behind = [(i, (i + 1) % count) for i in range(count)]
    return lax.ppermute(first, axis, ahead), lax.ppermute(last, axis, behind)


def swaps(near, far, axis):
    count = lax.axis_size(axis)
    odd = [(i, (i + (1 if i % 2 else -1)) % count) for i in range(count)]
    even = [(i, i ^ 1) for i in range(count)]
    near = lax.ppermute(near, axis, even)
    return lax.ppermute(far, axis, odd), near


def body(gas_fields, drop_mass, drop_temp, drop_speed, dest_first, cell_first, dest_second, cell_second):
    sectors = lax.axis_size("azim")
    _, count_z, count_a, radial = gas_fields.shape
    aspect = count_a * sectors / (2.0 * math.pi * radial)
    cells = count_z * count_a
    n1 = drop_mass.shape[0] // LANES
    n2 = cell_second.shape[0] // LANES
    gas = gas_fields.reshape(3, cells, radial)
    block = (sectors, 3 * SUB, LANES)
    z_edge = ((9, count_a, radial), F32)
    a_edge = ((9, count_z, radial), F32)
    planes = ((3, cells, radial), F32)
    cell_1 = cell_first.reshape(n1, LANES)
    cell_2 = cell_second.reshape(n2, LANES)

    out_1, source_1 = kernel(
        first_kernel,
        [(block, F32), ((3, n1, LANES), F32)],
        [pltpu.VMEM((3, cells, radial), F32)]
        + [pltpu.VMEM((n1, LANES), F32)] * 3
        + [pltpu.VMEM((n1, LANES), jnp.int32)] * 2
        + [pltpu.SemaphoreType.DMA((6,))]
        + [pltpu.VMEM((3, n1, LANES), F32), pltpu.VMEM((n1, LANES), jnp.int32), pltpu.VMEM((n1 * SUB, LANES), F32)],
        n_in=6,
        home=pltpu.HBM,
        limit=WHOLE_VMEM,
        cost=3.0,
    )(
        gas,
        drop_mass.reshape(n1, LANES),
        drop_temp.reshape(n1, LANES),
        drop_speed.reshape(n1, LANES),
        cell_1,
        dest_first.reshape(n1, LANES),
    )
    arrived_1 = lax.all_to_all(out_1, "azim", split_axis=0, concat_axis=0, tiled=True)
    added_1, far_z, near_z, first_a, last_a, slots_2 = kernel(
        lambda *refs: first_deposit_kernel(sectors, count_a, *refs),
        [planes, z_edge, z_edge, a_edge, a_edge, ((n2, LANES), jnp.int32)],
        n_in=4,
        cost=1.4,
    )(source_1, cell_1, gas, dest_second.reshape(n2, LANES))
    far_z, near_z = swaps(near_z, far_z, "axial")
    a_next, a_prev = shifts(first_a, last_a, "azim")

    middle, out_2, source_2 = kernel(
        lambda *refs: middle_kernel(aspect, *refs),
        [planes, (block, F32), ((3, n2, LANES), F32)],
        [pltpu.VMEM((3, n2, LANES), F32), pltpu.VMEM((n2 * SUB, LANES), F32)],
        n_in=9,
        cost=4.0,
    )(gas, added_1, far_z, near_z, a_next, a_prev, arrived_1, cell_2, slots_2)
    arrived_2 = lax.all_to_all(out_2, "azim", split_axis=0, concat_axis=0, tiled=True)
    (added_2,) = kernel(last_deposit_kernel, [planes], n_in=2)(source_2, cell_2)
    gas_next, drop_records = kernel(
        lambda *refs: last_kernel(aspect, *refs),
        [planes, ((6, n2 * LANES), F32)],
        [pltpu.VMEM((LANES, LANES), F32)],
        n_in=9,
        cost=1.8,
    )(gas, middle, added_2, far_z, near_z, a_next, a_prev, arrived_1, arrived_2)
    return gas_next.reshape(gas_fields.shape), drop_records


def solution(mesh):
    rows = P(("axial", "azim"))
    columns = P(("axial", "azim"), None)
    placed = (P(None, "axial", "azim", None), rows, rows, rows, columns, rows, columns, rows)
    return jax.shard_map(
        body,
        mesh=mesh,
        in_specs=placed,
        out_specs=(P(None, "axial", "azim", None), P(None, ("axial", "azim"))),
        check_vma=False,
    )
```

```python
import math

import jax
import jax.numpy as jnp
from jax import lax
from jax.experimental import pallas as pl
from jax.experimental.pallas import tpu as pltpu
from jax.sharding import PartitionSpec as P

DT_STEP = 0.01
TAU_HEAT = 0.04
TAU_MASS = 0.05
TAU_DRAG = 0.03
LATENT = 0.5
COUPLING = 1.0
FORCING = (0.0, 0.0, 4.0)
ADVECT = 0.16
RADIUS_FLOOR = 0.7
DIFFUSION = (0.2, 0.15, 0.17)
WALL_VALUES = (1.0, 0.0, 0.0)

F32 = jnp.float32
BF16 = jnp.bfloat16
LANES = 128
SUB = 8
VMEM_LIMIT = 40 << 20
WHOLE_VMEM = 60 << 20
COST_SCALE = 1.0


def iota(shape, dim):
    return lax.broadcasted_iota(jnp.int32, shape, dim)


def one_hot(row, size):
    hit = iota((size, row.shape[1]), 0) == row
    return jnp.where(hit, 1.0, 0.0).astype(BF16)


def halves(x):
    head = x.astype(BF16)
    return head, (x - head.astype(F32)).astype(BF16)


def wide_row(ref, j):
    return jnp.concatenate([ref[pl.ds(j, 1), :], ref[pl.ds(j + 1, 1), :]], axis=1)


def dot_nt(a, b):
    return lax.dot_general(a, b, (((1,), (1,)), ((), ())), preferred_element_type=F32)


def gas_table(planes):
    turned = [p.T for p in planes]
    parts = [jnp.concatenate(halves(t), axis=1) for t in turned]
    return jnp.concatenate(parts, axis=0), turned


def sample(table, cell_ref, out_ref):
    size = table.shape[1] // 2
    lanes_r = table.shape[0] // 3
    shift = lanes_r.bit_length() - 1
    for j in range(0, cell_ref.shape[0], 2):
        cell = wide_row(cell_ref, j)
        pick = one_hot(cell >> shift, size)
        mixed = jnp.dot(table, jnp.concatenate([pick, pick], axis=0), preferred_element_type=F32)
        here = iota((lanes_r, cell.shape[1]), 0) == (cell & (lanes_r - 1))
        for c in range(3):
            part = jnp.where(here, mixed[c * lanes_r : (c + 1) * lanes_r], 0.0)
            row = jnp.sum(part, axis=0, keepdims=True)
            out_ref[c, pl.ds(j, 1), :] = row[:, :LANES]
            out_ref[c, pl.ds(j + 1, 1), :] = row[:, LANES:]


def droplet_rates(states, gas, live):
    mass, temp, speed = states
    excess = 0.3 + 0.2 * jnp.tanh(temp) - gas[1]
    evaporate = mass * excess / TAU_MASS
    heating = gas[0] - temp
    drag = gas[2] - speed
    change = (
        -evaporate * live,
        (heating / TAU_HEAT - LATENT * excess / TAU_MASS) * live,
        drag / TAU_DRAG * live,
    )
    source = (
        -COUPLING * mass * heating / TAU_HEAT,
        COUPLING * evaporate,
        -COUPLING * mass * drag / TAU_DRAG,
    )
    return change, source


def deposit(source_ref, cell_ref, rows, lanes_r):
    shift = lanes_r.bit_length() - 1
    low = lanes_r // 2
    total = None
    for j in range(0, cell_ref.shape[0], 2):
        cell = wide_row(cell_ref, j)
        column = jnp.where((cell & low) > 0, rows, 0) + (cell >> shift)
        here = iota((low, cell.shape[1]), 0) == (cell & (low - 1))
        pairs = [halves(wide_row(source_ref.at[c], j)) for c in range(3)]
        spread = [
            jnp.where(here, pairs[c][part].astype(F32), 0.0) for part in range(2) for c in range(3)
        ]
        piece = dot_nt(jnp.concatenate(spread, axis=0).astype(BF16), one_hot(column, 2 * rows))
        total = piece if total is None else total + piece
    total = total[: 3 * low] + total[3 * low :]
    planes = [total[c * low : (c + 1) * low] for c in range(3)]
    return [jnp.concatenate([p[:, :rows], p[:, rows:]], axis=0).T for p in planes]


def slot_of(dest, sectors, capacity):
    n = dest.shape[0]
    hits = jnp.concatenate(
        [jnp.where(dest == t, 1.0, 0.0) for t in range(sectors)], axis=0
    ).astype(BF16)
    upto = jnp.where(iota((LANES, LANES), 0) <= iota((LANES, LANES), 1), 1.0, 0.0).astype(BF16)
    inside = jnp.dot(hits, upto, preferred_element_type=F32)
    every = jnp.dot(hits, jnp.ones((LANES, LANES), BF16), preferred_element_type=F32)
    before = jnp.where(iota((n, n), 1) < iota((n, n), 0), 1.0, 0.0).astype(BF16)
    rank = jnp.zeros(dest.shape, F32)
    for t in range(sectors):
        rows = slice(t * n, (t + 1) * n)
        carry = jnp.dot(before, every[rows].astype(BF16), preferred_element_type=F32)
        rank = rank + jnp.where(dest == t, inside[rows] + carry, 0.0)
    return dest * capacity + rank.astype(jnp.int32) - 1


def place(record_ref, slot_ref, out_ref):
    sectors = out_ref.shape[0]
    capacity = 2 * LANES
    total = None
    for j in range(0, slot_ref.shape[0], 2):
        slot = wide_row(slot_ref, j)
        sector = slot >> (capacity.bit_length() - 1)
        record = jnp.concatenate(
            [record_ref[pl.ds(SUB * j, SUB), :], record_ref[pl.ds(SUB * (j + 1), SUB), :]], axis=1
        )
        spread = [
            jnp.where(sector == t, part.astype(F32), 0.0)
            for part in halves(record)
            for t in range(sectors)
        ]
        piece = dot_nt(
            jnp.concatenate(spread, axis=0).astype(BF16), one_hot(slot & (capacity - 1), capacity)
        )
        total = piece if total is None else total + piece
    count = sectors * SUB
    total = total[:count] + total[count:]
    out_ref[:, :SUB, :] = total[:, :LANES].reshape(sectors, SUB, LANES)
    out_ref[:, SUB : 2 * SUB, :] = total[:, LANES:].reshape(sectors, SUB, LANES)


def near_rows(turned):
    return jnp.concatenate([t[:2] for t in turned] + [jnp.zeros((2, LANES), F32)], axis=0)


def send_near(out_ref, near):
    for t in range(out_ref.shape[0]):
        out_ref[t, 2 * SUB : 3 * SUB, :] = near


def columns_of(ref, c, at, count_z, count_a):
    return ref[c, pl.ds(at, count_z, stride=count_a), :]


def first_kernel(
    gas_hbm, mass_hbm, temp_hbm, speed_hbm, cell_hbm, dest_hbm,
    out, source,
    gas, mass, temp, speed, cell, dest, sems, gathered, slots, records,
):
    sectors = out.shape[0]
    loads = [
        pltpu.make_async_copy(a, b, sems.at[i])
        for i, (a, b) in enumerate(
            (
                (dest_hbm, dest),
                (gas_hbm, gas),
                (cell_hbm, cell),
                (mass_hbm, mass),
                (temp_hbm, temp),
                (speed_hbm, speed),
            )
        )
    ]
    for load in loads:
        load.start()
    records[...] = jnp.zeros(records.shape, F32)
    loads[0].wait()
    slots[...] = slot_of(dest[...], sectors, 2 * LANES)
    for load in loads[1:]:
        load.wait()
    table, turned = gas_table([gas[c] for c in range(3)])
    send_near(out, near_rows(turned))
    sample(table, cell, gathered)
    states = (mass[...], temp[...], speed[...])
    live = jnp.where(states[0] > 0, 1.0, 0.0)
    change, terms = droplet_rates(states, [gathered[c] for c in range(3)], live)
    n = cell.shape[0]
    for c in range(3):
        source[c] = terms[c]
        records[pl.ds(c, n, stride=SUB), :] = states[c] + DT_STEP * change[c]
        records[pl.ds(3 + c, n, stride=SUB), :] = states[c]
    place(records, slots, out)


def first_deposit_kernel(count_a, source, cell, gas, out, far_z, near_z, first_a, last_a):
    total = deposit(source, cell, out.shape[1], out.shape[2])
    end = out.shape[1]
    even = (lax.axis_index("axial") & 1) == 0
    for c in range(3):
        out[c] = total[c]
        first = [gas[c, :count_a, :], gas[c, count_a : 2 * count_a, :], total[c][:count_a]]
        last = [
            gas[c, end - count_a :, :],
            gas[c, end - 2 * count_a : end - count_a, :],
            total[c][end - count_a :],
        ]
        for i in range(3):
            near_z[3 * c + i] = jnp.where(even, last[i], first[i])
            far_z[3 * c + i] = jnp.where(even, first[i], last[i])
    count_z = first_a.shape[1]
    for c in range(3):
        for edge, at, inner in ((first_a, 0, 1), (last_a, count_a - 1, count_a - 2)):
            edge[3 * c] = columns_of(gas, c, at, count_z, count_a)
            edge[3 * c + 1] = columns_of(gas, c, inner, count_z, count_a)
            edge[3 * c + 2] = columns_of(out, c, at, count_z, count_a)


def slot_kernel(sectors, dest, after, slots):
    del after
    slots[...] = slot_of(dest[...], sectors, 2 * LANES)


def last_deposit_kernel(source, cell, out):
    total = deposit(source, cell, out.shape[1], out.shape[2])
    for c in range(3):
        out[c] = total[c]


def stencil(fields, following, preceding, right, left, near, added, aspect):
    shape = fields[0].shape
    pos = iota((1, 1, LANES), 2).astype(F32) + 0.5
    inverse = 1.0 / (12.0 * pos)
    geometry = aspect * aspect / jnp.maximum(pos / LANES, RADIUS_FLOOR) ** 2
    lane = iota(shape, 2)
    results = []
    for c in range(3):
        q = fields[c]
        edge = 2.0 * WALL_VALUES[c]
        near_0, near_1 = near[c]
        up = pltpu.roll(q, LANES - 1, 2)
        down = pltpu.roll(q, 1, 2)
        up_2 = pltpu.roll(q, LANES - 2, 2)
        down_2 = pltpu.roll(q, 2, 2)
        plus_one = jnp.where(lane == LANES - 1, edge - q, up)
        plus_two = jnp.where(
            lane == LANES - 1, edge - down, jnp.where(lane == LANES - 2, edge - up, up_2)
        )
        minus_one = jnp.where(lane == 0, near_0, down)
        minus_two = jnp.where(lane == 0, near_1, jnp.where(lane == 1, near_0, down_2))
        laplace = (16.0 * (plus_one + minus_one) - 30.0 * q - plus_two - minus_two) / 12.0
        laplace = laplace + (8.0 * (plus_one - minus_one) - plus_two + minus_two) * inverse
        laplace = laplace + geometry * (right[c] + left[c] - 2.0 * q)
        laplace = laplace + (following[c] + preceding[c] - 2.0 * q) / 16.0
        results.append(
            q
            + DIFFUSION[c] * laplace
            - ADVECT * fields[2] * (following[c] - preceding[c])
            + DT_STEP * (added[c] + FORCING[c])
        )
    return results


def sides(fields, right_edge, left_edge):
    count_a = fields[0].shape[1]
    column = iota(fields[0].shape, 1)
    pairs = [
        (
            jnp.where(column == count_a - 1, right_edge[c], pltpu.roll(q, count_a - 1, 1)),
            jnp.where(column == 0, left_edge[c], pltpu.roll(q, 1, 1)),
        )
        for c, q in enumerate(fields)
    ]
    return [p[0] for p in pairs], [p[1] for p in pairs]


def between(q, z_prev, z_next):
    return (
        jnp.concatenate([q[1:], z_next[None]], axis=0),
        jnp.concatenate([z_prev[None], q[:-1]], axis=0),
    )


def near_columns(near):
    return jnp.concatenate([near, jnp.zeros((LANES - SUB, LANES), F32)], axis=0).T


def column_blocks(across, count_z, count_a):
    return [
        [across[:, 2 * c + i : 2 * c + i + 1].reshape(count_z, count_a, 1) for i in range(2)]
        for c in range(3)
    ]


def across_axis(sectors):
    return lax.axis_index("azim") ^ (sectors // 2)


def outer_planes(near_z, far_z):
    even = (lax.axis_index("axial") & 1) == 0
    count = range(near_z.shape[0])
    return (
        [jnp.where(even, near_z[i], far_z[i]) for i in count],
        [jnp.where(even, far_z[i], near_z[i]) for i in count],
    )


def middle_kernel(
    aspect, gas, added, far_z, near_z, a_next, a_prev, arrived, cell, slots,
    middle, out, source, gathered, records,
):
    count_z, count_a = a_next.shape[1], near_z.shape[1]
    shape = (count_z, count_a, LANES)
    sectors = arrived.shape[0]
    z_next, z_prev = outer_planes(near_z, far_z)
    across = near_columns(arrived[across_axis(sectors), 2 * SUB :, :])
    fields = [gas[c].reshape(shape) for c in range(3)]
    pairs = [between(fields[c], z_prev[3 * c], z_next[3 * c]) for c in range(3)]
    results = stencil(
        fields,
        [p[0] for p in pairs],
        [p[1] for p in pairs],
        *sides(
            fields,
            [a_next[3 * c].reshape(count_z, 1, LANES) for c in range(3)],
            [a_prev[3 * c].reshape(count_z, 1, LANES) for c in range(3)],
        ),
        column_blocks(across, count_z, count_a),
        [added[c].reshape(shape) for c in range(3)],
        aspect,
    )
    for c in range(3):
        middle[c] = results[c].reshape(middle.shape[1:])
    table, turned = gas_table([middle[c] for c in range(3)])
    sample(table, cell, gathered)

    outer = [planes[3 * c] for c in range(3) for planes in (z_prev, z_next)]
    rest = jnp.zeros((LANES - len(outer) * count_a, LANES), F32)
    outer_near = jnp.concatenate(outer + [rest], axis=0).T[:2]
    near = jnp.concatenate([t[:2] for t in turned] + [outer_near], axis=0)
    spare = jnp.zeros((SUB - len(outer), LANES), F32)
    to_right = jnp.concatenate([p[count_a - 1 :] for p in outer] + [spare], axis=0)
    to_left = jnp.concatenate([p[:1] for p in outer] + [spare], axis=0)
    right, across_to = neighbour(1, sectors), across_axis(sectors)
    for t in range(sectors):
        out[t, 2 * SUB :, :] = jnp.where(across_to == t, near, jnp.where(right == t, to_right, to_left))

    for half in range(2):
        values = [arrived[:, half * SUB + c, :] for c in range(6)]
        now, anchor = values[:3], values[3:]
        live = jnp.where(anchor[0] > 0, 1.0, 0.0)
        rows = pl.ds(half, sectors, stride=2)
        change, terms = droplet_rates(now, [gathered[c, rows, :] for c in range(3)], live)
        for c in range(3):
            source[c, rows, :] = terms[c]
            final = 0.75 * anchor[c] + 0.25 * (now[c] + DT_STEP * change[c])
            records[pl.ds(half * SUB + c, sectors, stride=2 * SUB), :] = final
            records[pl.ds(half * SUB + 3 + c, sectors, stride=2 * SUB), :] = anchor[c]
        for c in range(6, SUB):
            records[pl.ds(half * SUB + c, sectors, stride=2 * SUB), :] = jnp.zeros((sectors, LANES), F32)
    place(records, slots, out)


def neighbour(step, sectors):
    return (lax.axis_index("azim") + step + sectors) % sectors


def last_kernel(
    aspect, gas, middle, added, far_z, near_z, a_next, a_prev, earlier, arrived,
    out, records, turned_near,
):
    count_a = near_z.shape[1]
    count_z = gas.shape[1] // count_a
    sectors = arrived.shape[0]
    shape = (count_z, count_a, LANES)
    end = gas.shape[1]
    z_next, z_prev = outer_planes(near_z, far_z)
    across = near_columns(arrived[across_axis(sectors), 2 * SUB :, :])
    ahead, behind = neighbour(1, sectors), neighbour(-1, sectors)
    corner_next = arrived[ahead, 2 * SUB :, :]
    corner_prev = arrived[behind, 2 * SUB :, :]

    def both(before, after):
        return jnp.concatenate([before[None], after[None]], axis=0)

    outer = [both(z_prev[3 * c], z_next[3 * c]) for c in range(3)]
    planes = stencil(
        outer,
        [both(gas[c, :count_a, :], z_next[3 * c + 1]) for c in range(3)],
        [both(z_prev[3 * c + 1], gas[c, end - count_a :, :]) for c in range(3)],
        *sides(
            outer,
            [corner_next[2 * c : 2 * c + 2].reshape(2, 1, LANES) for c in range(3)],
            [corner_prev[2 * c : 2 * c + 2].reshape(2, 1, LANES) for c in range(3)],
        ),
        [
            [
                across[2 * c * count_a : 2 * (c + 1) * count_a, 6 + i : 7 + i].reshape(2, count_a, 1)
                for i in range(2)
            ]
            for c in range(3)
        ],
        [both(z_prev[3 * c + 2], z_next[3 * c + 2]) for c in range(3)],
        aspect,
    )
    columns = []
    for edge, corner, sector, at in (
        (a_prev, corner_prev, behind, count_a - 1),
        (a_next, corner_next, ahead, 0),
    ):
        turned_near[...] = near_columns(earlier[sector ^ (sectors // 2), 2 * SUB :, :])
        near = turned_near[pl.ds(at, count_z, stride=count_a), :]
        own = [columns_of(gas, c, count_a - 1 - at, count_z, count_a) for c in range(3)]
        inner = [edge[3 * c + 1] for c in range(3)]
        fields = [edge[3 * c] for c in range(3)]
        following = [
            jnp.concatenate([fields[c][1:], corner[2 * c + 1 : 2 * c + 2]], axis=0) for c in range(3)
        ]
        preceding = [
            jnp.concatenate([corner[2 * c : 2 * c + 1], fields[c][:-1]], axis=0) for c in range(3)
        ]
        columns.append(
            stencil(
                [f[None] for f in fields],
                [f[None] for f in following],
                [f[None] for f in preceding],
                [f[None] for f in own],
                [f[None] for f in inner],
                [[near[None, :, 2 * c + i : 2 * c + i + 1] for i in range(2)] for c in range(3)],
                [edge[3 * c + 2][None] for c in range(3)],
                aspect,
            )
        )
    left, right = columns
    fields = [middle[c].reshape(shape) for c in range(3)]
    pairs = [between(fields[c], planes[c][0], planes[c][1]) for c in range(3)]
    results = stencil(
        fields,
        [p[0] for p in pairs],
        [p[1] for p in pairs],
        *sides(
            fields,
            [right[c].reshape(count_z, 1, LANES) for c in range(3)],
            [left[c].reshape(count_z, 1, LANES) for c in range(3)],
        ),
        column_blocks(across, count_z, count_a),
        [added[c].reshape(shape) for c in range(3)],
        aspect,
    )
    for c in range(3):
        out[c] = 0.75 * gas[c] + 0.25 * results[c].reshape(out.shape[1:])
    for s in range(sectors):
        for half in range(2):
            at = (2 * s + half) * LANES
            records[:, at : at + LANES] = arrived[s, half * SUB : half * SUB + 6, :]


def kernel(body, outs, scratch=(), smem=(), n_in=0, home=pltpu.VMEM, limit=VMEM_LIMIT, cost=1.0):
    def spec(i):
        return pl.BlockSpec(memory_space=pltpu.SMEM if i in smem else home)

    return pl.pallas_call(
        body,
        out_shape=[jax.ShapeDtypeStruct(s, d) for s, d in outs],
        in_specs=[spec(i) for i in range(n_in)],
        out_specs=[pl.BlockSpec(memory_space=pltpu.VMEM) for _ in outs],
        scratch_shapes=list(scratch),
        compiler_params=pltpu.CompilerParams(vmem_limit_bytes=limit),
        cost_estimate=pl.CostEstimate(flops=int(cost * 1e9 * COST_SCALE), bytes_accessed=0, transcendentals=0),
    )


def shifts(first, last, axis):
    count = lax.axis_size(axis)
    ahead = [((i + 1) % count, i) for i in range(count)]
    behind = [(i, (i + 1) % count) for i in range(count)]
    return lax.ppermute(first, axis, ahead), lax.ppermute(last, axis, behind)


def swaps(near, far, axis):
    count = lax.axis_size(axis)
    odd = [(i, (i + (1 if i % 2 else -1)) % count) for i in range(count)]
    even = [(i, i ^ 1) for i in range(count)]
    near = lax.ppermute(near, axis, even)
    return lax.ppermute(far, axis, odd), near


def body(gas_fields, drop_mass, drop_temp, drop_speed, dest_first, cell_first, dest_second, cell_second):
    sectors = lax.axis_size("azim")
    _, count_z, count_a, radial = gas_fields.shape
    aspect = count_a * sectors / (2.0 * math.pi * radial)
    cells = count_z * count_a
    n1 = drop_mass.shape[0] // LANES
    n2 = cell_second.shape[0] // LANES
    gas = gas_fields.reshape(3, cells, radial)
    block = (sectors, 3 * SUB, LANES)
    z_edge = ((9, count_a, radial), F32)
    a_edge = ((9, count_z, radial), F32)
    planes = ((3, cells, radial), F32)
    cell_1 = cell_first.reshape(n1, LANES)
    cell_2 = cell_second.reshape(n2, LANES)

    out_1, source_1 = kernel(
        first_kernel,
        [(block, F32), ((3, n1, LANES), F32)],
        [pltpu.VMEM((3, cells, radial), F32)]
        + [pltpu.VMEM((n1, LANES), F32)] * 3
        + [pltpu.VMEM((n1, LANES), jnp.int32)] * 2
        + [pltpu.SemaphoreType.DMA((6,))]
        + [pltpu.VMEM((3, n1, LANES), F32), pltpu.VMEM((n1, LANES), jnp.int32), pltpu.VMEM((n1 * SUB, LANES), F32)],
        n_in=6,
        home=pltpu.HBM,
        limit=WHOLE_VMEM,
        cost=3.0,
    )(
        gas,
        drop_mass.reshape(n1, LANES),
        drop_temp.reshape(n1, LANES),
        drop_speed.reshape(n1, LANES),
        cell_1,
        dest_first.reshape(n1, LANES),
    )
    arrived_1 = lax.all_to_all(out_1, "azim", split_axis=0, concat_axis=0, tiled=True)
    added_1, far_z, near_z, first_a, last_a = kernel(
        lambda *refs: first_deposit_kernel(count_a, *refs),
        [planes, z_edge, z_edge, a_edge, a_edge],
        n_in=3,
        cost=1.4,
    )(source_1, cell_1, gas)
    (slots_2,) = kernel(
        lambda *refs: slot_kernel(sectors, *refs), [((n2, LANES), jnp.int32)], n_in=2
    )(dest_second.reshape(n2, LANES), added_1)
    far_z, near_z = swaps(near_z, far_z, "axial")
    a_next, a_prev = shifts(first_a, last_a, "azim")

    middle, out_2, source_2 = kernel(
        lambda *refs: middle_kernel(aspect, *refs),
        [planes, (block, F32), ((3, n2, LANES), F32)],
        [pltpu.VMEM((3, n2, LANES), F32), pltpu.VMEM((n2 * SUB, LANES), F32)],
        n_in=9,
        cost=4.0,
    )(gas, added_1, far_z, near_z, a_next, a_prev, arrived_1, cell_2, slots_2)
    arrived_2 = lax.all_to_all(out_2, "azim", split_axis=0, concat_axis=0, tiled=True)
    (added_2,) = kernel(last_deposit_kernel, [planes], n_in=2)(source_2, cell_2)
    gas_next, drop_records = kernel(
        lambda *refs: last_kernel(aspect, *refs),
        [planes, ((6, n2 * LANES), F32)],
        [pltpu.VMEM((LANES, LANES), F32)],
        n_in=9,
        cost=1.8,
    )(gas, middle, added_2, far_z, near_z, a_next, a_prev, arrived_1, arrived_2)
    return gas_next.reshape(gas_fields.shape), drop_records


def solution(mesh):
    rows = P(("axial", "azim"))
    columns = P(("axial", "azim"), None)
    placed = (P(None, "axial", "azim", None), rows, rows, rows, columns, rows, columns, rows)
    return jax.shard_map(
        body,
        mesh=mesh,
        in_specs=placed,
        out_specs=(P(None, "axial", "azim", None), P(None, ("axial", "azim"))),
        check_vma=False,
    )
```
